128 devices in a mesh: rows: 16 (over y, z), keys: 8 (over x, core).
Axes of the slice: x: 4, y: 4, z: 4, core: 2. Of those that a mesh axis runs over, the one named last changes fastest.
Arguments:
- queries: bfloat16 [32768, 128], P('rows'), may hold values from -12 to 12
- keys_in: bfloat16 [32768, 128], P(('rows', 'keys')), may hold values from -12 to 12
- c_proj: bfloat16 [32768, 64], P('rows'), may hold values from -6 to 6
- b_proj: bfloat16 [32768, 64], P(('rows', 'keys')), may hold values from -6 to 6
- log_decay: float32 [32768], P(('rows', 'keys')), as said below
- segments: int32 [32768], P(('rows', 'keys')), may hold values from 0 to 3, never falling along the last dimension, each value on 1 to 16384 neighbouring positions
Outputs:
- grad_c: float32 [32768, 64], P(('rows', 'keys'))
- grad_b: float32 [32768, 64], P(('rows', 'keys'))
- grad_decay: float32 [32768], P(('rows', 'keys'))
The draws below stay inside these ranges and needn't reach their ends.
Inputs may be any that keep to these rules, and one draw needn't show every extreme that they name: `log_decay`: negative at every position.
All inputs are finite; a program needn't handle non-finite values.
Results may differ from the reference program's by a relative error of at most 0.00055.
Values may be sent and summed in bfloat16 or wider, within the bound.
No kernel may reach another device: no remote copies, remote signals or barrier semaphores. Data moves between devices by JAX's collectives and lax.ppermute only.
A program may use at most 128 MiB of HBM per device.

```python
import math
import jax
import jax.numpy as jnp
import numpy as np
from jax import lax

HEAD = 128
STATE = 64
KB = 256
SEQ = 32768
N_KEYS = 8


def teacher_pair(key):
    base = jax.random.fold_in(key, 5)
    key_q, key_k = jax.random.split(base, 2)
    query = jnp.clip(1.7 * jax.random.normal(key_q, (SEQ, HEAD), jnp.float32), -8.0, 8.0)
    keyed = jnp.clip(1.7 * jax.random.normal(key_k, (SEQ, HEAD), jnp.float32), -8.0, 8.0)
    return (query, keyed)


def draw_queries(key, part):
    return teacher_pair(key)[0].astype(jnp.bfloat16)


def draw_keys_in(key, part):
    return teacher_pair(key)[1].astype(jnp.bfloat16)


def draw_log_decay(key, part):
    key_a, key_b, key_c, key_e, key_f = jax.random.split(jax.random.fold_in(key, 11), 5)
    rate = jnp.exp(jax.random.uniform(key_a, (SEQ,), jnp.float32, math.log(0.15), math.log(0.75)))
    base = -rate / SEQ
    spots = jax.random.randint(key_b, (4,), 0, SEQ)
    drops = jax.random.uniform(key_c, (4,), jnp.float32, 0.22, 0.69)
    many = max(SEQ // 64, 1)
    small_spots = jax.random.randint(key_e, (many,), 0, SEQ)
    small_drops = jax.random.uniform(key_f, (many,), jnp.float32, 0.001, 0.005)
    return base.at[spots].add(-drops).at[small_spots].add(-small_drops)


def levels(key, dims, cuts, low, high):
    def one(dim, shards_of):
        heights = jax.random.uniform(jax.random.fold_in(jax.random.fold_in(key, 6), dim), (shards_of,), jnp.float32, low / len(cuts), high / len(cuts))
        return jnp.repeat(jnp.exp(heights), dims[dim] // shards_of).reshape((-1,) + (1,) * (len(dims) - dim - 1))

    loudness = one(*cuts[0])
    for cut in cuts[1:]:
        loudness = loudness * one(*cut)
    return loudness


def split_up(number_of, total, most, lean):
    loads = [(1 << 20) // math.isqrt(rank ** lean) + 1 for rank in range(2, number_of + 1)]
    spare, holding = total - most - (number_of - 1), [1] * (number_of - 1)
    while spare > 0:
        movable = [i for i in range(number_of - 1) if holding[i] < most]
        whole, remaining = sum([loads[i] for i in movable]), spare
        for i in movable:
            extra = min(most - holding[i], max(1, remaining * loads[i] // whole), spare)
            holding[i] = holding[i] + extra
            spare = spare - extra
    return np.array([most] + holding)


def ragged_sizes(stream_key, amount, total, bound, skew):
    if amount == 2:
        one = jax.random.randint(stream_key, (), max(1, total - bound), min(bound, total - 1) + 1)
        return jnp.stack([one, total - one])
    sizes = jnp.asarray(split_up(amount, total, bound, skew), jnp.int32)
    twos = (amount - 1) // 2
    giver, sink = sizes[1:1 + 2 * twos:2], sizes[2:2 + 2 * twos:2]
    slack = jnp.minimum(giver - 1, bound - sink)
    moved = jax.random.randint(jax.random.fold_in(stream_key, 1), (twos,), 0, 1 << 20) % (slack + 1)
    sizes = sizes.at[1:1 + 2 * twos:2].set(giver - moved).at[2:2 + 2 * twos:2].set(sink + moved)
    return sizes[jax.random.permutation(jax.random.fold_in(stream_key, 2), amount)]


def scatter_about(rng, dims, width, reach, cuts=(), held_as=jnp.bfloat16):
    result = jax.random.normal(rng, dims, jnp.float32) * width
    if len(cuts) > 0:
        result = levels(rng, dims, cuts, -0.22, 0.18) * result
    return jnp.clip(result, min=-reach, max=reach).astype(held_as)


def setup_inputs(seed: int = 0) -> dict:
    key_list = jax.random.split(jax.random.key(seed), 7)
    queries = draw_queries(jax.random.fold_in(key_list[6], 71), 0)
    keys_in = draw_keys_in(jax.random.fold_in(key_list[6], 71), 0)
    c_proj = scatter_about(key_list[2], (SEQ, STATE), 1.0, 6.0, ((0, 16),))
    b_proj = scatter_about(key_list[3], (SEQ, STATE), 1.0, 6.0, ((0, 128),))
    log_decay = draw_log_decay(jax.random.fold_in(key_list[6], 71), 0)
    segments = jnp.searchsorted(jnp.cumsum(ragged_sizes(key_list[5], 4, SEQ, SEQ // 2, 0)), jnp.arange(SEQ), side="right").astype(jnp.int32)
    return dict(queries=queries, keys_in=keys_in, c_proj=c_proj, b_proj=b_proj, log_decay=log_decay, segments=segments)


def reference(queries, keys_in, c_proj, b_proj, log_decay, segments):
    scale = HEAD ** -0.5
    block = KB * N_KEYS
    count = SEQ // block
    cum = jnp.cumsum(log_decay)
    places = jnp.arange(SEQ, dtype=jnp.int32)
    b_wide = b_proj.astype(jnp.float32)

    def one_block(carry, index):
        grad_keys, column = carry
        start = (index * block).astype(jnp.int32)
        query = lax.dynamic_slice_in_dim(queries, start, block, 0)
        cproj = lax.dynamic_slice_in_dim(c_proj, start, block, 0)
        qcum = lax.dynamic_slice_in_dim(cum, start, block, 0)
        qlab = lax.dynamic_slice_in_dim(segments, start, block, 0)
        qpos = start + jnp.arange(block, dtype=jnp.int32)
        visible = (places[None, :] <= qpos[:, None]) & (segments[None, :] == qlab[:, None])
        scores = jnp.dot(query, keys_in.T, preferred_element_type=jnp.float32) * scale
        top = jnp.max(jnp.where(visible, scores, -jnp.inf), axis=1)
        total = jnp.sum(jnp.where(visible, jnp.exp(scores - top[:, None]), 0.0), axis=1)
        attn = jnp.where(visible, jnp.exp(scores - top[:, None]) / total[:, None], 0.0)
        weight = jnp.where(visible, jnp.exp(qcum[:, None] - cum[None, :]), 0.0)
        inner = jnp.dot(cproj, b_proj.T, preferred_element_type=jnp.float32)
        differ = 2.0 * (weight * inner / SEQ - attn)
        slope = differ * weight
        along = slope * inner
        grad_rows = jnp.dot(slope, b_wide, precision=lax.Precision.HIGHEST, preferred_element_type=jnp.float32)
        grad_keys = grad_keys + jnp.dot(slope.T, cproj.astype(jnp.float32), precision=lax.Precision.HIGHEST,
                                        preferred_element_type=jnp.float32)
        column = column + jnp.sum(along, axis=0)
        return (grad_keys, column), (grad_rows, jnp.sum(along, axis=1))

    start_carry = (jnp.zeros((SEQ, STATE), jnp.float32), jnp.zeros((SEQ,), jnp.float32))
    (grad_b, column), (grad_c, rowsum) = lax.scan(one_block, start_carry, jnp.arange(count, dtype=jnp.int32))
    grad_c = grad_c.reshape(SEQ, STATE)
    rowsum = rowsum.reshape(SEQ)
    lead = rowsum - column
    tail = jnp.cumsum(lead[::-1])[::-1]
    return grad_c, grad_b, tail / SEQ
```

```python
import functools

import jax
import jax.numpy as jnp
from jax import lax
from jax.experimental import pallas as pl
from jax.experimental.pallas import tpu as pltpu
from jax.sharding import PartitionSpec as P

ROWS = "rows"
KEYS = "keys"
BOTH = ("rows", "keys")
BACK = 8
NROWS = 16
NKEYS = 8
KB = 256
QR = KB * NKEYS
HEAD = 128
STATE = 64
SEQ = QR * NROWS
LOG2E = 1.4426950408889634
CS = HEAD**-0.5 * LOG2E
NEG = -1e30
TQ = 512
F32 = jnp.float32
BF16 = jnp.bfloat16
HI = lax.Precision.HIGHEST


def dot(a, b):
    return jnp.dot(a, b, preferred_element_type=F32)


def dotx(a, b):
    return jnp.dot(a, b, precision=HI, preferred_element_type=F32)


def iota(shape, dim):
    return lax.broadcasted_iota(jnp.int32, shape, dim)


def split2(x):
    hi = x.astype(BF16)
    lo = (x - hi.astype(F32)).astype(BF16)
    return hi, lo


def split3(x):
    hi = x.astype(BF16).astype(F32)
    mid = (x - hi).astype(BF16).astype(F32)
    return hi, mid, x - hi - mid


def total_of(x):
    return jnp.sum(jnp.sum(x, axis=0, keepdims=True), axis=1, keepdims=True)


def columns(row):
    return jnp.concatenate(
        [
            jnp.transpose(jnp.broadcast_to(row[:, h * 128 : (h + 1) * 128], (128, 128)))
            for h in range(2)
        ],
        axis=0,
    )


def prep_kernel(x_ref, k_ref, b_ref, msg_ref, row_ref, own_ref):
    kk = lax.axis_index(KEYS)
    ld = jnp.concatenate([x_ref[a, 0:2, :] for a in range(NKEYS)], axis=0)
    sg = jnp.concatenate([x_ref[a, 2:4, :] for a in range(NKEYS)], axis=0)
    upper = (iota((128, 128), 0) <= iota((128, 128), 1)).astype(F32)
    inside = dotx(ld, upper)
    tot = jnp.broadcast_to(inside[:, 127:128], (16, 128))
    lower = (iota((16, 16), 1) < iota((16, 16), 0)).astype(F32)
    pre = inside + dotx(lower, tot)
    rowtotal = pre[15:16, 127:128]
    row_ref[...] = jnp.zeros_like(row_ref)
    row_ref[0:1, :] = jnp.concatenate([pre[a : a + 1] for a in range(16)], axis=1)
    row_ref[1:2, :] = jnp.concatenate([sg[a : a + 1] for a in range(16)], axis=1)

    def own(arr):
        line = iota((16, 128), 0)
        return columns(
            jnp.concatenate(
                [
                    jnp.sum(jnp.where(line == 2 * kk + h, arr, 0.0), axis=0, keepdims=True)
                    for h in range(2)
                ],
                axis=1,
            )
        )

    precol, segcol = own(pre), own(sg)
    parts = (*split3(rowtotal - precol), segcol, *split3(rowtotal))
    lane = iota((KB, 128), 1)
    wide = jnp.concatenate([b_ref[...].astype(F32), jnp.zeros((KB, 64), F32)], axis=1)
    for n, part in enumerate(parts):
        wide = jnp.where(lane == 64 + n, part, wide)
    wide = jnp.where(lane == 71, 1.0, wide)
    msg_ref[:, 0:128] = k_ref[...]
    msg_ref[:, 128:256] = wide.astype(BF16)
    own_ref[...] = jnp.where(lane == 0, precol, segcol)


def diag_kernel(msg_ref, own_ref, row_ref, q_ref, c_ref,
                qt_ref, ct_ref, st_ref, od_ref, os_ref, gb_ref, h_ref):
    kk = lax.axis_index(KEYS)
    qt_ref[...] = jnp.transpose(q_ref[...])
    ctf = jnp.transpose(c_ref[...].astype(F32))
    ct_ref[...] = ctf.astype(BF16)
    seg = row_ref[1:2, :]
    u = jnp.where(seg == seg[:, 0:1], jnp.exp2(LOG2E * row_ref[0:1, :]), 0.0)
    h_ref[...] = dotx(ctf * (u * u), c_ref[...].astype(F32))
    gb_ref[...] = jnp.zeros_like(gb_ref)
    st_ref[...] = jnp.zeros_like(st_ref)
    b = msg_ref[:, 128:192]
    bt = jnp.transpose(b.astype(F32)).astype(BF16)
    prej = own_ref[:, 0:1]
    segj = own_ref[:, 1:2]
    for q in range(NKEYS):
        sl = slice(q * KB, (q + 1) * KB)

        @pl.when(q < kk)
        def _():
            st_ref[0:1, sl] = jnp.full((1, KB), NEG, F32)
            od_ref[:, sl] = jnp.zeros((STATE, KB), F32)
            os_ref[:, sl] = jnp.zeros((STATE, KB), F32)

        @pl.when(q >= kk)
        def _():
            s = dot(msg_ref[:, 0:128], qt_ref[:, sl])
            ahead = (q - kk) * KB
            mask = (segj == row_ref[1:2, sl]) & (
                iota((KB, KB), 0) <= iota((KB, KB), 1) + ahead
            )
            s = jnp.where(mask, s * CS, NEG)
            top = jnp.max(s, axis=0, keepdims=True)
            e = jnp.where(mask, jnp.exp2(s - top), 0.0)
            st_ref[0:1, sl] = top
            st_ref[1:2, sl] = jnp.sum(e, axis=0, keepdims=True)
            w = jnp.where(mask, jnp.exp2(LOG2E * (row_ref[0:1, sl] - prej)), 0.0)
            hi, lo = split2(e * w)
            od_ref[:, sl] = dot(bt, hi) + dot(bt, lo)
            inner = dot(b, ct_ref[:, sl])
            hi, lo = split2(w * w * inner * (2.0 / SEQ))
            os_ref[:, sl] = dot(bt, hi) + dot(bt, lo)
            gb_ref[...] += dot(hi, c_ref[sl, :]) + dot(lo, c_ref[sl, :])


def meta_of(msg_ref):
    meta = msg_ref[:, 128:256].astype(F32)
    sfx = meta[:, 64:65] + meta[:, 65:66] + meta[:, 66:67]
    first = meta[0:1, :]
    rowtotal = first[:, 68:69] + first[:, 69:70] + first[:, 70:71]
    return meta[:, 0:64], sfx, meta[:, 67:68], rowtotal, meta[:, 71:72]


def tiles_in(row_ref):
    seg = row_ref[1:2, :]
    count = jnp.sum(jnp.where(seg == seg[:, 0:1], 1.0, 0.0))
    return (count.astype(jnp.int32) + (TQ - 1)) // TQ


def stats_kernel(*refs):
    msgs = refs[:BACK]
    (qt_ref, ct_ref, row_ref, st_ref, h_ref,
     send_ref, ou_ref, os_ref, mref_ref, d_ref, ast_ref,
     qaug, kaug, o_acc, m_acc, l_acc, g_acc) = refs[BACK:]
    seg = row_ref[1:2, :]
    doc = seg[:, 0:1]
    inside = seg == doc
    qaug[0:128, :] = qt_ref[...]
    line = iota((128, QR), 0)
    qaug[128:256, :] = jnp.where(
        line == 0, 1.0, jnp.where(line == 1, jnp.where(inside, 0.0, NEG), 0.0)
    ).astype(BF16)
    m_acc[...] = st_ref[0:1, :]
    l_acc[...] = st_ref[1:2, :]
    o_acc[...] = jnp.zeros_like(o_acc)
    g_acc[...] = jnp.zeros_like(g_acc)
    mref_ref[...] = jnp.full_like(mref_ref, NEG)
    d_ref[...] = jnp.zeros_like(d_ref)
    ast_ref[...] = jnp.zeros_like(ast_ref)
    tiles = tiles_in(row_ref)
    off = jnp.zeros((1, 1), F32)
    for n in range(BACK):
        b, sfx, segj, rowtotal, valid = meta_of(msgs[n])
        seen = (segj == doc) & (valid > 0.0)
        here = off
        off = off + rowtotal

        @pl.when(jnp.max(jnp.where(seen, 1.0, 0.0)) > 0.0)
        def _():
            v = jnp.where(seen, jnp.exp2(LOG2E * (sfx + here)), 0.0)
            kaug[:, 0:128] = msgs[n][:, 0:128]
            lane = iota((KB, 128), 1)
            kaug[:, 128:256] = jnp.where(
                lane == 0, jnp.where(seen, 0.0, NEG), jnp.where(lane == 1, 1.0, 0.0)
            ).astype(BF16)
            bv = b * v
            bhi = bv.astype(BF16).astype(F32)
            both = jnp.transpose(jnp.concatenate([bhi, bv - bhi], axis=1))
            bt = both.astype(BF16)
            g = dotx(both[0:64] + both[64:128], bv)
            g_acc[...] += g
            ast_ref[n : n + 1, :] = jnp.broadcast_to(total_of(g * h_ref[...]), (1, 128))

            def tile(t, carry):
                sl = pl.ds(pl.multiple_of(t * TQ, TQ), TQ)
                s = dot(kaug[...], qaug[:, sl])
                old = m_acc[:, sl]
                new = jnp.maximum(old, jnp.max(s, axis=0, keepdims=True) * CS)
                a = jnp.exp2(old - new)
                e = jnp.exp2(s * CS - new)
                l_acc[:, sl] = l_acc[:, sl] * a + jnp.sum(e, axis=0, keepdims=True)
                m_acc[:, sl] = new
                hi, lo = split2(e)
                add = dot(bt, hi) + dot(bt, lo)
                o_acc[:, sl] = o_acc[:, sl] * a + add
                mref_ref[n : n + 1, sl] = new
                d_ref[n : n + 1, sl] = jnp.sum(
                    (add[0:64] + add[64:128]) * ct_ref[:, sl].astype(F32), axis=0, keepdims=True
                )
                return carry

            lax.fori_loop(0, tiles, tile, 0)

    for k in range(NKEYS):
        send_ref[k, 0:1, :] = m_acc[...]
        send_ref[k, 1:2, :] = l_acc[...]
    u = jnp.where(inside, jnp.exp2(LOG2E * row_ref[0:1, :]), 0.0)
    ou_ref[...] = jnp.where(inside, u * (o_acc[0:64, :] + o_acc[64:128, :]), 0.0)
    os_ref[...] = dotx(g_acc[...], ct_ref[...].astype(F32) * (u * u)) * (2.0 / SEQ)


def scale_kernel(recv_ref, st_ref, row_ref, ct_ref, ou_ref, os_ref, od_ref, osd_ref,
                 mref_ref, d_ref, ast_ref, gc_ref, scal_ref, lse_ref):
    kk = lax.axis_index(KEYS)
    tops = [recv_ref[k, 0:1, :] for k in range(NKEYS)]
    top = functools.reduce(jnp.maximum, tops)
    total = sum(recv_ref[k, 1:2, :] * jnp.exp2(tops[k] - top) for k in range(NKEYS))
    lse = top + jnp.log2(total)
    lse_ref[...] = jnp.broadcast_to(lse, (8, QR))
    mine = recv_ref[pl.ds(kk, 1), 0:1, :].reshape(1, QR)
    f = jnp.exp2(mine - lse)
    fd = jnp.exp2(st_ref[0:1, :] - lse)
    ctf = ct_ref[...].astype(F32)
    near = -2.0 * fd * od_ref[...] + osd_ref[...]
    gc = -2.0 * f * ou_ref[...] + os_ref[...] + near
    for k in range(NKEYS):
        gc_ref[k] = gc[:, k * KB : (k + 1) * KB]
    along = jnp.sum(ctf * gc, axis=0, keepdims=True)
    lane = iota((1, 128), 1)
    out = jnp.where(lane == 0, total_of(ctf * near), 0.0)
    seg = row_ref[1:2, :]
    u = jnp.where(seg == seg[:, 0:1], jnp.exp2(LOG2E * row_ref[0:1, :]), 0.0)
    far = jnp.where(u > 0.0, jnp.exp2(mref_ref[...] - lse) * u * d_ref[...], 0.0)
    far = -2.0 * jnp.sum(far, axis=1, keepdims=True) + (2.0 / SEQ) * ast_ref[:, 0:1]
    for n in range(BACK):
        out = jnp.where(lane == n + 1, far[n : n + 1, :], out)
    for q in range(NKEYS):
        part = jnp.sum(along[:, q * KB : (q + 1) * KB], axis=1, keepdims=True)
        out = jnp.where(lane == 16 + q, part, out)
    scal_ref[...] = jnp.broadcast_to(out, (NROWS * NKEYS, 128))


def packed(g):
    return jnp.concatenate([g[0:128], g[128:256]], axis=1)


def grad_kernel(*refs):
    msgs = refs[:BACK]
    (msg_ref, own_ref, row_ref, qt_ref, c_ref, lse_ref, h_ref, gbd_ref) = refs[BACK : BACK + 8]
    outs = refs[BACK + 8 : BACK + 8 + BACK]
    gb_ref, qaug, kaug, g_acc = refs[BACK + 8 + BACK :]
    kk = lax.axis_index(KEYS)
    seg = row_ref[1:2, :]
    doc = seg[:, 0:1]
    inside = seg == doc
    base = LOG2E * row_ref[0:1, :] - lse_ref[0:1, :]
    qaug[0:128, :] = qt_ref[...]
    line = iota((128, QR), 0)
    rows = jnp.where(line < 3, 1.0, 0.0)
    for n, part in enumerate(split3(jnp.where(inside, base * (1.0 / CS), NEG))):
        rows = jnp.where(line == 3 + n, part, rows)
    qaug[128:256, :] = rows.astype(BF16)
    tiles = tiles_in(row_ref)
    off = jnp.zeros((1, 1), F32)
    for n in range(BACK):
        b, sfx, segj, rowtotal, valid = meta_of(msgs[n])
        seen = (segj == doc) & (valid > 0.0)
        here = off
        off = off + rowtotal
        active = jnp.max(jnp.where(seen, 1.0, 0.0)) > 0.0

        @pl.when(jnp.logical_not(active))
        def _():
            outs[n][...] = jnp.zeros_like(outs[n])

        @pl.when(active)
        def _():
            e = LOG2E * (sfx + here)
            v = jnp.where(seen, jnp.exp2(e), 0.0)
            kaug[:, 0:128] = msgs[n][:, 0:128]
            lane = iota((KB, 128), 1)
            cols = jnp.where((lane >= 3) & (lane < 6), 1.0, 0.0)
            for i, part in enumerate(split3(jnp.where(seen, e * (1.0 / CS), NEG))):
                cols = jnp.where(lane == i, part, cols)
            kaug[:, 128:256] = cols.astype(BF16)
            g_acc[...] = jnp.zeros_like(g_acc)

            def tile(t, carry):
                sl = pl.ds(pl.multiple_of(t * TQ, TQ), TQ)
                p = jnp.exp2(CS * dot(kaug[...], qaug[:, sl]))
                hi, lo = split2(p)
                c = c_ref[sl, :]
                g_acc[...] += dot(hi, c) + dot(lo, c)
                return carry

            lax.fori_loop(0, tiles, tile, 0)
            g = -2.0 * g_acc[...] + (2.0 / SEQ) * (v * v) * dotx(b, h_ref[...])
            outs[n][...] = packed(g)

    g_acc[...] = jnp.zeros_like(g_acc)
    prej = own_ref[:, 0:1]
    segj = own_ref[:, 1:2]
    for q in range(NKEYS):
        sl = slice(q * KB, (q + 1) * KB)

        @pl.when(q >= kk)
        def _():
            s = dot(msg_ref[:, 0:128], qt_ref[:, sl])
            mask = (segj == row_ref[1:2, sl]) & (
                iota((KB, KB), 0) <= iota((KB, KB), 1) + (q - kk) * KB
            )
            p = jnp.where(mask, jnp.exp2(s * CS + base[:, sl] - LOG2E * prej), 0.0)
            hi, lo = split2(p)
            g_acc[...] += dot(hi, c_ref[sl, :]) + dot(lo, c_ref[sl, :])

    gb_ref[...] = gbd_ref[...] - 2.0 * g_acc[...]


def final_kernel(*refs):
    got = refs[:BACK]
    gb_ref, gc_ref, scal_ref, b_ref, c_ref, out_c, out_b, out_d = refs[BACK:]
    row, kk = lax.axis_index(ROWS), lax.axis_index(KEYS)
    both = functools.reduce(jnp.add, [g[...] for g in got])
    gb = gb_ref[...] + jnp.concatenate([both[:, 0:64], both[:, 64:128]], axis=0)
    gc = jnp.transpose(functools.reduce(jnp.add, [gc_ref[k] for k in range(NKEYS)]))
    out_b[...] = gb
    out_c[...] = gc
    c = c_ref[pl.ds(pl.multiple_of(kk * KB, KB), KB), :].astype(F32)
    lead = c * gc - b_ref[...].astype(F32) * gb
    line = lax.dot_general(
        jnp.ones((8, STATE), F32), lead, (((1,), (1,)), ((), ())),
        precision=HI, preferred_element_type=F32,
    )
    after = (iota((KB, KB), 0) >= iota((KB, KB), 1)).astype(F32)
    local = dotx(line, after)
    me = row * NKEYS + kk
    dev, lane = iota((128, 128), 0), iota((128, 128), 1)
    chunk = jnp.where(lane >= 16, (dev // NKEYS) * NKEYS + lane - 16, dev - lane * NKEYS)
    sign = jnp.where(lane <= BACK, -1.0, jnp.where((lane >= 16) & (lane < 24), 1.0, 0.0))
    tail = total_of(jnp.where(chunk > me, sign * scal_ref[...], 0.0))
    out_d[...] = (local[0:1, :] + tail) * (1.0 / SEQ)


def sds(shape, dtype=F32):
    return jax.ShapeDtypeStruct(shape, dtype)


def on_device(queries, keys_in, c_proj, b_proj, log_decay, segments):
    line = jnp.concatenate([log_decay, segments.astype(F32)]).reshape(4, 128)
    x = lax.all_to_all(jnp.broadcast_to(line, (NKEYS, 4, 128)), KEYS, 0, 0, tiled=True)
    msg, rowmeta, own = pl.pallas_call(
        prep_kernel,
        out_shape=(sds((KB, 256), BF16), sds((8, QR)), sds((KB, 128))),
        name="prep",
    )(x, keys_in, b_proj)
    msgs = [
        lax.ppermute(msg, ROWS, [(r, r + s) for r in range(NROWS - s)])
        for s in range(1, BACK + 1)
    ]
    qt, ct, st, od, osd, gbd, h = pl.pallas_call(
        diag_kernel,
        out_shape=(
            sds((HEAD, QR), BF16), sds((STATE, QR), BF16), sds((8, QR)),
            sds((STATE, QR)), sds((STATE, QR)), sds((KB, STATE)), sds((STATE, STATE)),
        ),
        name="diag",
    )(msg, own, rowmeta, queries, c_proj)
    send, ou, os, mref, d, ast = pl.pallas_call(
        stats_kernel,
        out_shape=(
            sds((NKEYS, 2, QR)), sds((STATE, QR)), sds((STATE, QR)),
            sds((BACK, QR)), sds((BACK, QR)), sds((BACK, 128)),
        ),
        scratch_shapes=[
            pltpu.VMEM((256, QR), BF16), pltpu.VMEM((KB, 256), BF16),
            pltpu.VMEM((128, QR), F32), pltpu.VMEM((1, QR), F32), pltpu.VMEM((1, QR), F32),
            pltpu.VMEM((STATE, STATE), F32),
        ],
        name="stats",
    )(*msgs, qt, ct, rowmeta, st, h)
    recv = lax.all_to_all(send, KEYS, 0, 0, tiled=True)
    gc, scal, lse = pl.pallas_call(
        scale_kernel,
        out_shape=(sds((NKEYS, STATE, KB)), sds((NROWS * NKEYS, 128)), sds((8, QR))),
        name="scale",
    )(recv, st, rowmeta, ct, ou, os, od, osd, mref, d, ast)
    gc = lax.all_to_all(gc, KEYS, 0, 0, tiled=True)
    scal = lax.all_to_all(scal, BOTH, 0, 0, tiled=True)
    grads = pl.pallas_call(
        grad_kernel,
        out_shape=(*[sds((128, 128))] * BACK, sds((KB, STATE))),
        scratch_shapes=[
            pltpu.VMEM((256, QR), BF16), pltpu.VMEM((KB, 256), BF16), pltpu.VMEM((KB, STATE), F32),
        ],
        name="grad",
    )(*msgs, msg, own, rowmeta, qt, c_proj, lse, h, gbd)
    back = [
        lax.ppermute(grads[s - 1], ROWS, [(r + s, r) for r in range(NROWS - s)])
        for s in range(1, BACK + 1)
    ]
    out_c, out_b, out_d = pl.pallas_call(
        final_kernel,
        out_shape=(sds((KB, STATE)), sds((KB, STATE)), sds((1, KB))),
        name="final",
    )(*back, grads[BACK], gc, scal, b_proj, c_proj)
    return out_c, out_b, out_d.reshape(KB)


def solution(mesh):
    return jax.shard_map(
        on_device,
        mesh=mesh,
        in_specs=(
            P(ROWS, None), P(BOTH, None), P(ROWS, None), P(BOTH, None), P(BOTH), P(BOTH),
        ),
        out_specs=(P(BOTH, None), P(BOTH, None), P(BOTH)),
        check_vma=False,
    )
```

```python
import functools

import jax
import jax.numpy as jnp
from jax import lax
from jax.experimental import pallas as pl
from jax.experimental.pallas import tpu as pltpu
from jax.sharding import PartitionSpec as P

ROWS = "rows"
KEYS = "keys"
BOTH = ("rows", "keys")
BACK = 8
NROWS = 16
NKEYS = 8
KB = 256
QR = KB * NKEYS
HEAD = 128
STATE = 64
SEQ = QR * NROWS
LOG2E = 1.4426950408889634
CS = HEAD**-0.5 * LOG2E
NEG = -1e30
TQ = 512
MSG = KB + 128 + 32
F32 = jnp.float32
BF16 = jnp.bfloat16
HI = lax.Precision.HIGHEST


def dot(a, b):
    return jnp.dot(a, b, preferred_element_type=F32)


def dotx(a, b):
    return jnp.dot(a, b, precision=HI, preferred_element_type=F32)


def iota(shape, dim):
    return lax.broadcasted_iota(jnp.int32, shape, dim)


def split2(x):
    hi = x.astype(BF16)
    lo = (x - hi.astype(F32)).astype(BF16)
    return hi, lo


def split3(x):
    hi = x.astype(BF16).astype(F32)
    mid = (x - hi).astype(BF16).astype(F32)
    return hi, mid, x - hi - mid


def total_of(x):
    return jnp.sum(jnp.sum(x, axis=0, keepdims=True), axis=1, keepdims=True)


def dot_nt(a, b):
    return lax.dot_general(a, b, (((1,), (1,)), ((), ())), preferred_element_type=F32)


def stacked_rows(rows, height, width):
    line = iota((height, width), 0)
    out = jnp.zeros((height, width), F32)
    for n, row in rows:
        out = jnp.where(line == n, row, out)
    return out


def columns_of(rows):
    wide = jnp.concatenate([rows, jnp.zeros((112, KB), F32)], axis=0)
    return jnp.transpose(wide)[:, 0:16]


def left_three(x):
    hi, lo = split2(x)
    return jnp.concatenate([hi, hi, lo], axis=1)


def right_three(x):
    hi, lo = split2(x)
    return jnp.concatenate([hi, lo, hi], axis=0)


def row_factor(row_ref):
    seg = row_ref[1:2, :]
    inside = seg == seg[:, 0:1]
    return inside, jnp.where(inside, jnp.exp2(LOG2E * row_ref[0:1, :]), 0.0)


def local_prefix(ld):
    upper = (iota((128, 128), 0) <= iota((128, 128), 1)).astype(F32)
    inside = dotx(jnp.concatenate([ld, jnp.zeros((6, 128), F32)], axis=0), upper)
    first = jnp.broadcast_to(inside[0:1, 127:128], (1, 128))
    second = jnp.broadcast_to(inside[1:2, 127:128], (1, 128))
    return (inside[0:1], inside[1:2] + first), first + second


def send_kernel(ld_ref, seg_ref, k_ref, bt_ref, out_ref, msg_ref):
    label = seg_ref[...].astype(F32)
    for k in range(NKEYS):
        out_ref[k, 0:2, :] = ld_ref[...]
        out_ref[k, 2:4, :] = label
    pre, total = local_prefix(ld_ref[...])
    msg_ref[0:KB, :] = k_ref[...]
    for h in range(2):
        rows = (*split3(total - pre[h]), label[h : h + 1], *split3(total), jnp.ones((1, 128), F32))
        msg_ref[KB + 64 * h : KB + 64 * (h + 1), :] = bt_ref[:, h * 128 : (h + 1) * 128]
        msg_ref[KB + 128 + 16 * h : KB + 144 + 16 * h, :] = stacked_rows(
            enumerate(rows), 16, 128
        ).astype(BF16)


def diag_kernel(x_ref, k_ref, bt_ref, q_ref, ct_ref,
                row_ref, qaug_ref, kaug_ref, st_ref, os_ref, gb_ref, h_ref):
    kk = lax.axis_index(KEYS)
    ld = jnp.concatenate([x_ref[a, 0:2, :] for a in range(NKEYS)], axis=0)
    sg = jnp.concatenate([x_ref[a, 2:4, :] for a in range(NKEYS)], axis=0)
    upper = (iota((128, 128), 0) <= iota((128, 128), 1)).astype(F32)
    within = dotx(ld, upper)
    tot = jnp.broadcast_to(within[:, 127:128], (16, 128))
    lower = (iota((16, 16), 1) < iota((16, 16), 0)).astype(F32)
    pre = within + dotx(lower, tot)
    row_ref[...] = jnp.zeros_like(row_ref)
    row_ref[0:1, :] = jnp.concatenate([pre[a : a + 1] for a in range(16)], axis=1)
    row_ref[1:2, :] = jnp.concatenate([sg[a : a + 1] for a in range(16)], axis=1)

    def own(arr):
        line = iota((16, 128), 0)
        halves = [
            jnp.sum(jnp.where(line == 2 * kk + h, arr, 0.0), axis=0, keepdims=True)
            for h in range(2)
        ]
        return jnp.concatenate(halves, axis=1)

    own_pre, own_seg = own(pre), own(sg)
    seg = row_ref[1:2, :]
    inside, u = row_factor(row_ref)
    qaug_ref[0:128, :] = jnp.transpose(q_ref[...])
    doc_rows = [(10 + n, jnp.where(seg == float(n), 0.0, NEG)) for n in range(4)]
    qaug_ref[128:144, :] = stacked_rows(
        [(3, 1.0), (4, jnp.where(inside, 0.0, NEG)), *doc_rows], 16, QR
    ).astype(BF16)
    qaug_ref[144:256, :] = jnp.zeros((112, QR), BF16)
    rows = list(enumerate(split3(own_pre * (-LOG2E / CS))))
    rows += [(7 + n, 1.0) for n in range(3)]
    rows += [(10 + n, jnp.where(own_seg == float(n), 1.0, 0.0)) for n in range(4)]
    rows += [(14, own_pre), (15, own_seg)]
    cols = columns_of(stacked_rows(rows, 16, KB))
    prej, segj = cols[:, 14:15], cols[:, 15:16]
    lane = iota((KB, 16), 1)
    kaug_ref[:, 0:128] = k_ref[...]
    kaug_ref[:, 128:256] = jnp.zeros((KB, 128), BF16)
    kaug_ref[:, 128:144] = jnp.where(lane < 14, cols, 0.0).astype(BF16)
    hi, lo = split2(ct_ref[...].astype(F32) * (u * u))
    h_ref[...] = dot_nt(hi, ct_ref[...]) + dot_nt(lo, ct_ref[...])
    gb_ref[...] = jnp.zeros_like(gb_ref)
    st_ref[0:1, :] = jnp.full((1, QR), NEG, F32)
    st_ref[1:2, :] = jnp.ones((1, QR), F32)
    st_ref[2:8, :] = jnp.zeros((6, QR), F32)
    os_ref[...] = jnp.zeros_like(os_ref)
    bt = bt_ref[...]
    b = jnp.transpose(bt.astype(F32)).astype(BF16)

    def chunk(q, carry):
        sl = pl.ds(pl.multiple_of(q * KB, KB), KB)
        causal = iota((KB, KB), 0) <= iota((KB, KB), 1) + (q - kk) * KB
        c = ct_ref[:, sl]
        inner = dot(b, c)
        s = jnp.where(causal, dot(kaug_ref[...], qaug_ref[:, sl]), NEG)
        top = jnp.max(s, axis=0, keepdims=True) * CS
        e = jnp.exp2(s * CS - top)
        st_ref[0:1, sl] = top
        st_ref[1:2, sl] = jnp.sum(e, axis=0, keepdims=True)
        w = jnp.where(
            causal & (segj == row_ref[1:2, sl]),
            jnp.exp2(LOG2E * (row_ref[0:1, sl] - prej)), 0.0,
        )
        wi = w * inner
        st_ref[2:3, sl] = jnp.sum(e * wi, axis=0, keepdims=True)
        hi, lo = split2(w * wi * (2.0 / SEQ))
        os_ref[:, sl] = dot(bt, hi) + dot(bt, lo)
        gb_ref[...] += dot_nt(c, hi) + dot_nt(c, lo)
        return carry

    lax.fori_loop(kk, NKEYS, chunk, 0)


def tiles_in(row_ref):
    seg = row_ref[1:2, :]
    count = jnp.sum(jnp.where(seg == seg[:, 0:1], 1.0, 0.0))
    return (count.astype(jnp.int32) + (TQ - 1)) // TQ


def after(pos, many, tiles):
    n, t = pos
    wrap = t + 1 >= tiles
    n = jnp.where(wrap, n + 1, n)
    return jnp.where(n >= many, BACK, n), jnp.where(wrap, 0, t + 1)


def lanes(pos):
    return pl.ds(pl.multiple_of(pos[1] * TQ, TQ), TQ)


def stats_kernel(*refs):
    msgs = refs[:BACK]
    (qaug, ct_ref, row_ref, st_ref, h_ref,
     send_ref, mref_ref, d_ref, gs_ref, kaug, bts_ref, gst_ref, nb_ref,
     bl, cc, m_acc, l_acc, s_a, s_b, i_a, i_b) = refs[BACK:]
    doc = row_ref[1:2, 0:1]
    m_acc[...] = st_ref[0:1, :]
    l_acc[...] = st_ref[1:2, :]
    mref_ref[...] = jnp.full_like(mref_ref, NEG)
    d_ref[...] = jnp.zeros_like(d_ref)
    gs_ref[...] = jnp.zeros_like(gs_ref)
    gst_ref[...] = jnp.zeros_like(gst_ref)
    cc[0:64, :] = ct_ref[...]
    cc[64:128, :] = ct_ref[...]
    lane = iota((KB, 128), 1)
    kaug[BACK, :, 0:128] = jnp.zeros((KB, 128), BF16)
    kaug[BACK, :, 128:256] = jnp.where((lane == 0) | (lane == 3), NEG, 0.0).astype(BF16)
    bts_ref[BACK] = jnp.zeros((STATE, KB), BF16)
    bl[BACK] = jnp.zeros((KB, 128), BF16)
    h_left = left_three(h_ref[...])
    count = jnp.int32(0)
    lane1 = iota((1, 128), 1)
    totals = jnp.zeros((1, 128), F32)
    for n in range(BACK):
        msg = msgs[n]
        meta = jnp.concatenate(
            [msg[KB + 128 : KB + 144, :], msg[KB + 144 : KB + 160, :]], axis=1
        ).astype(F32)
        seen = (meta[3:4] == doc) & (meta[7:8] > 0.0)
        here = LOG2E * (meta[0:1] + meta[1:2] + meta[2:3])
        totals = jnp.where(
            lane1 == n, meta[4:5, 0:128] + meta[5:6, 0:128] + meta[6:7, 0:128], totals
        )
        active = jnp.max(jnp.where(seen, 1.0, 0.0)) > 0.0
        count = count + active.astype(jnp.int32)

        @pl.when(active)
        def _():
            v = jnp.where(seen, jnp.exp2(here), 0.0)
            rows = list(enumerate(split3(jnp.where(seen, here * (1.0 / CS), NEG))))
            rows += [(3, jnp.where(seen, 0.0, NEG)), (4, 1.0), (5, 1.0), (6, 1.0)]
            kaug[n, :, 0:128] = msg[0:KB, :]
            kaug[n, :, 128:256] = jnp.zeros((KB, 128), BF16)
            kaug[n, :, 128:144] = columns_of(stacked_rows(rows, 16, KB)).astype(BF16)
            bt = jnp.concatenate([msg[KB : KB + 64, :], msg[KB + 64 : KB + 128, :]], axis=1)
            bts_ref[n] = bt
            bv = bt.astype(F32) * v
            hi = bv.astype(BF16).astype(F32)
            both = jnp.concatenate([hi, bv - hi], axis=0)
            bl[n] = jnp.transpose(both).astype(BF16)
            both = both.astype(BF16)
            g = dot_nt(both, both)
            gs_ref[n] = g[0:64, 0:64] + g[0:64, 64:128] + g[64:128, 0:64] + g[64:128, 64:128]
            gst_ref[n] = dot(h_left, right_three(bv)) * v * (2.0 / SEQ)

    nb_ref[0] = count
    tiles = tiles_in(row_ref)

    def scores(pos, s_buf, i_buf):
        s_buf[...] = dot(kaug[pos[0]], qaug[:, lanes(pos)])
        i_buf[...] = dot(bl[pos[0]], cc[:, lanes(pos)])

    def work(pos, s_buf, i_buf):
        sl = lanes(pos)
        old = m_acc[:, sl]
        new = jnp.maximum(old, jnp.max(s_buf[...], axis=0, keepdims=True) * CS)
        e = jnp.exp2(s_buf[...] * CS - new)
        l_acc[:, sl] = l_acc[:, sl] * jnp.exp2(old - new) + jnp.sum(e, axis=0, keepdims=True)
        m_acc[:, sl] = new
        mref_ref[pl.ds(pos[0], 1), sl] = new
        d_ref[pl.ds(pos[0], 1), sl] = jnp.sum(e * i_buf[...], axis=0, keepdims=True)

    @pl.when(count > 0)
    def _():
        first = (jnp.int32(0), jnp.int32(0))
        scores(first, s_a, i_a)

        def step(_, pos):
            second = after(pos, count, tiles)
            third = after(second, count, tiles)
            scores(second, s_b, i_b)
            work(pos, s_a, i_a)
            scores(third, s_a, i_a)
            work(second, s_b, i_b)
            return third

        lax.fori_loop(0, (count * tiles + 1) // 2, step, first)

    lse = m_acc[...] + jnp.log2(l_acc[...])
    for k in range(NKEYS):
        send_ref[k, 0:1, :] = lse
        send_ref[k, 1:2, 0:128] = totals


def scale_kernel(recv_ref, st_ref, row_ref, ct_ref, osd_ref, mref_ref, d_ref, gs_ref, h_ref,
                 scal_ref, aug_ref, os_ref, eo_ref):
    kk = lax.axis_index(KEYS)
    parts = [recv_ref[k, 0:1, :] for k in range(NKEYS)]
    top = functools.reduce(jnp.maximum, parts)
    lse = top + jnp.log2(sum(jnp.exp2(p - top) for p in parts))
    totals = [recv_ref[k, 1:2, 0:128] for k in range(NKEYS)]
    later = sum(jnp.where(k > kk, totals[k], 0.0) for k in range(NKEYS))
    rowtot = sum(totals)
    run = jnp.zeros((1, 1), F32)
    offs = []
    for n in range(BACK):
        offs.append((n, jnp.broadcast_to(later[:, n : n + 1] + run, (1, 128))))
        run = run + rowtot[:, n : n + 1]
    eo = jnp.exp2(LOG2E * stacked_rows(offs, 8, 128))
    eo_ref[0:8, :] = jnp.concatenate([eo] * 4, axis=1)
    eo_ref[8:16, :] = jnp.zeros((8, TQ), F32)
    seg = row_ref[1:2, :]
    inside, u = row_factor(row_ref)
    beta = (LOG2E * row_ref[0:1, :] - lse) * (1.0 / CS)
    rows = [(n, 1.0) for n in range(3)]
    rows += [(4 + n, part) for n, part in enumerate(split3(jnp.where(inside, beta, NEG)))]
    rows += [(7 + n, part) for n, part in enumerate(split3(beta))]
    rows += [(10 + n, jnp.where(seg == float(n), 0.0, NEG)) for n in range(4)]
    aug_ref[...] = stacked_rows(rows, 16, QR).astype(BF16)
    ctf = ct_ref[...].astype(F32)
    h = h_ref[...]
    g_all = jnp.zeros((STATE, STATE), F32)
    ast = []
    for n in range(BACK):
        weighted = gs_ref[n] * (eo[n : n + 1, 0:64] * eo[n : n + 1, 0:64])
        g_all = g_all + weighted
        ast.append(total_of(weighted * h) * (2.0 / SEQ))
    osd = osd_ref[...]
    os = osd + dot(left_three(g_all * (2.0 / SEQ)), right_three(ctf * (u * u)))
    os_ref[...] = os
    fd = -2.0 * jnp.exp2(st_ref[0:1, :] - lse) * st_ref[2:3, :]
    near = fd + jnp.sum(ctf * osd, axis=0, keepdims=True)
    far = jnp.where(inside, jnp.exp2(mref_ref[0:8, :] - lse) * u * d_ref[0:8, :], 0.0)
    far = -2.0 * eo[:, 0:1] * far
    along = fd + jnp.sum(ctf * os, axis=0, keepdims=True) + jnp.sum(far, axis=0, keepdims=True)
    far = jnp.sum(far, axis=1, keepdims=True)
    lane = iota((1, 128), 1)
    out = jnp.where(lane == 0, total_of(near), 0.0)
    for n in range(BACK):
        out = jnp.where(lane == n + 1, far[n : n + 1, :] + ast[n], out)
    for q in range(NKEYS):
        part = jnp.sum(along[:, q * KB : (q + 1) * KB], axis=1, keepdims=True)
        out = jnp.where(lane == 16 + q, part, out)
    scal_ref[...] = jnp.broadcast_to(out, (NROWS * NKEYS, 128))


def grad_kernel(nb_ref, kaug, bts, gst_ref, qaug_ref, aug_ref, ct_ref, row_ref, os_ref, eo_ref,
                kd_ref, btd_ref, gbd_ref, *rest):
    outs = rest[:BACK]
    gb_ref, gc_ref, qaug, g_acc, o_acc, s_a, s_b, h_a, h_b, l_a, l_b = rest[BACK:]
    kk = lax.axis_index(KEYS)
    qaug[...] = qaug_ref[...]
    qaug[128:144, :] = aug_ref[...]
    g_acc[...] = jnp.zeros_like(g_acc)
    o_acc[...] = jnp.zeros_like(o_acc)
    count = nb_ref[0]
    tiles = tiles_in(row_ref)

    def scores(pos, s_buf):
        s_buf[...] = dot(kaug[pos[0]], qaug[:, lanes(pos)])

    def weigh(s_buf, h_buf, l_buf):
        hi, lo = split2(jnp.exp2(CS * s_buf[...]))
        h_buf[...] = hi
        l_buf[...] = lo

    def add(pos, h_buf, l_buf):
        sl = lanes(pos)
        c, b = ct_ref[:, sl], bts[pos[0]]
        g = dot_nt(c, h_buf[...]) + dot_nt(c, l_buf[...])
        g_acc[pl.ds(pos[0], 1)] += g.reshape(1, STATE, KB)
        o = dot(b, h_buf[...]) + dot(b, l_buf[...])
        o_acc[:, sl] += o * eo_ref[pl.ds(pos[0], 1), :]

    @pl.when(count > 0)
    def _():
        first = (jnp.int32(0), jnp.int32(0))
        scores(first, s_a)
        weigh(s_a, h_a, l_a)
        second = after(first, count, tiles)
        scores(second, s_b)

        def step(_, carry):
            pos, second = carry[:2], carry[2:]
            third = after(second, count, tiles)
            fourth = after(third, count, tiles)
            add(pos, h_a, l_a)
            weigh(s_b, h_b, l_b)
            scores(third, s_a)
            add(second, h_b, l_b)
            weigh(s_a, h_a, l_a)
            scores(fourth, s_b)
            return (*third, *fourth)

        lax.fori_loop(0, (count * tiles + 1) // 2, step, (*first, *second))

    for n in range(BACK):

        @pl.when(n < count)
        def _():
            e = eo_ref[n : n + 1, 0:KB]
            outs[n][...] = gst_ref[n] * (e * e) - 2.0 * e * g_acc[n]

        @pl.when(n >= count)
        def _():
            outs[n][...] = jnp.zeros_like(outs[n])

    gb_ref[...] = gbd_ref[...]

    def chunk(q, carry):
        sl = pl.ds(pl.multiple_of(q * KB, KB), KB)
        causal = iota((KB, KB), 0) <= iota((KB, KB), 1) + (q - kk) * KB
        p = jnp.where(causal, jnp.exp2(CS * dot(kd_ref[...], qaug[:, sl])), 0.0)
        hi, lo = split2(p)
        c, b = ct_ref[:, sl], btd_ref[...]
        gb_ref[...] -= 2.0 * (dot_nt(c, hi) + dot_nt(c, lo))
        o_acc[:, sl] += dot(b, hi) + dot(b, lo)
        return carry

    lax.fori_loop(kk, NKEYS, chunk, 0)
    for k in range(NKEYS):
        sl = slice(k * KB, (k + 1) * KB)
        gc_ref[k] = os_ref[:, sl] - 2.0 * o_acc[:, sl]


def final_kernel(*refs):
    got = refs[:BACK]
    gb_ref, gc_ref, scal_ref, bt_ref, ct_ref, out_c, out_b, out_d = refs[BACK:]
    row, kk = lax.axis_index(ROWS), lax.axis_index(KEYS)
    gb = functools.reduce(jnp.add, [g[...] for g in got]) + gb_ref[...]
    gc = functools.reduce(jnp.add, [gc_ref[k] for k in range(NKEYS)])
    out_b[...] = gb
    out_c[...] = gc
    c = ct_ref[:, pl.ds(pl.multiple_of(kk * KB, KB), KB)].astype(F32)
    lead = jnp.sum(c * gc - bt_ref[...].astype(F32) * gb, axis=0, keepdims=True)
    later = (iota((KB, KB), 0) >= iota((KB, KB), 1)).astype(F32)
    local = dotx(jnp.broadcast_to(lead, (8, KB)), later)
    me = row * NKEYS + kk
    dev, lane = iota((128, 128), 0), iota((128, 128), 1)
    chunk = jnp.where(lane >= 16, (dev // NKEYS) * NKEYS + lane - 16, dev - lane * NKEYS)
    sign = jnp.where(lane <= BACK, -1.0, jnp.where((lane >= 16) & (lane < 24), 1.0, 0.0))
    tail = total_of(jnp.where(chunk > me, sign * scal_ref[...], 0.0))
    out_d[...] = (local[0:1, :] + tail) * (1.0 / SEQ)


def sds(shape, dtype=F32):
    return jax.ShapeDtypeStruct(shape, dtype)


def vmem():
    return pl.BlockSpec(memory_space=pltpu.VMEM)


def smem():
    return pl.BlockSpec(memory_space=pltpu.SMEM)


def on_device(queries, keys_in, c_proj, b_proj, log_decay, segments):
    ct, bt = c_proj.T, b_proj.T
    x, msg = pl.pallas_call(
        send_kernel, out_shape=(sds((NKEYS, 4, 128)), sds((MSG, 128), BF16)), name="send"
    )(log_decay.reshape(2, 128), segments.reshape(2, 128), keys_in, bt)
    x = lax.all_to_all(x, KEYS, 0, 0, tiled=True)
    msgs = [
        lax.ppermute(msg, ROWS, [(r, r + s) for r in range(NROWS - s)])
        for s in range(1, BACK + 1)
    ]
    rowmeta, qaug, kd, st, osd, gbd, h = pl.pallas_call(
        diag_kernel,
        out_shape=(
            sds((8, QR)), sds((256, QR), BF16), sds((KB, 256), BF16), sds((8, QR)),
            sds((STATE, QR)), sds((STATE, KB)), sds((STATE, STATE)),
        ),
        name="diag",
    )(x, keys_in, bt, queries, ct)
    send, mref, d, gs, kaug, bts, gst, nb = pl.pallas_call(
        stats_kernel,
        out_shape=(
            sds((NKEYS, 2, QR)), sds((16, QR)), sds((16, QR)), sds((BACK, STATE, STATE)),
            sds((BACK + 1, KB, 256), BF16), sds((BACK + 1, STATE, KB), BF16),
            sds((BACK, STATE, KB)), sds((1,), jnp.int32),
        ),
        out_specs=(*[vmem()] * 7, smem()),
        scratch_shapes=[
            pltpu.VMEM((BACK + 1, KB, 128), BF16), pltpu.VMEM((128, QR), BF16),
            pltpu.VMEM((1, QR), F32), pltpu.VMEM((1, QR), F32),
            *[pltpu.VMEM((KB, TQ), F32)] * 4,
        ],
        name="stats",
    )(*msgs, qaug, ct, rowmeta, st, h)
    recv = lax.all_to_all(send, KEYS, 0, 0, tiled=True)
    scal, aug, os, eo = pl.pallas_call(
        scale_kernel,
        out_shape=(
            sds((NROWS * NKEYS, 128)), sds((16, QR), BF16), sds((STATE, QR)), sds((16, TQ)),
        ),
        name="scale",
    )(recv, st, rowmeta, ct, osd, mref, d, gs, h)
    scal = lax.all_to_all(scal, BOTH, 0, 0, tiled=True)
    *grads, gb, gc = pl.pallas_call(
        grad_kernel,
        in_specs=[smem(), *[vmem()] * 12],
        out_shape=(*[sds((STATE, KB))] * (BACK + 1), sds((NKEYS, STATE, KB))),
        scratch_shapes=[
            pltpu.VMEM((256, QR), BF16), pltpu.VMEM((BACK + 1, STATE, KB), F32),
            pltpu.VMEM((STATE, QR), F32),
            *[pltpu.VMEM((KB, TQ), F32)] * 2, *[pltpu.VMEM((KB, TQ), BF16)] * 4,
        ],
        name="grad",
    )(nb, kaug, bts, gst, qaug, aug, ct, rowmeta, os, eo, kd, bt, gbd)
    gc = lax.all_to_all(gc, KEYS, 0, 0, tiled=True)
    back = [
        lax.ppermute(g, ROWS, [(r + s, r) for r in range(NROWS - s)])
        for s, g in enumerate(grads, 1)
    ]
    out_c, out_b, out_d = pl.pallas_call(
        final_kernel,
        out_shape=(sds((STATE, KB)), sds((STATE, KB)), sds((1, KB))),
        name="final",
    )(*back, gb, gc, scal, bt, ct)
    return out_c.T, out_b.T, out_d.reshape(KB)


def solution(mesh):
    return jax.shard_map(
        on_device,
        mesh=mesh,
        in_specs=(
            P(ROWS, None), P(BOTH, None), P(ROWS, None), P(BOTH, None), P(BOTH), P(BOTH),
        ),
        out_specs=(P(BOTH, None), P(BOTH, None), P(BOTH)),
        check_vma=False,
    )
```

```python
import functools

import jax
import jax.numpy as jnp
from jax import lax
from jax.experimental import pallas as pl
from jax.experimental.pallas import tpu as pltpu
from jax.sharding import PartitionSpec as P


ROWS = "rows"
KEYS = "keys"
BOTH = ("rows", "keys")
BACK = 8
HOPS = BACK // 2
HALF = BACK // 2
NROWS = 16
NKEYS = 8
KB = 256
QR = KB * NKEYS
HEAD = 128
STATE = 64
SEQ = QR * NROWS
LOG2E = 1.4426950408889634
CS = HEAD**-0.5 * LOG2E
NEG = -1e30
TQ = 512
MSG = KB + 128 + 32
F32 = jnp.float32
BF16 = jnp.bfloat16
HI = lax.Precision.HIGHEST


def dot(a, b):
    return jnp.dot(a, b, preferred_element_type=F32)


def dotx(a, b):
    return jnp.dot(a, b, precision=HI, preferred_element_type=F32)


def iota(shape, dim):
    return lax.broadcasted_iota(jnp.int32, shape, dim)


def split2(x):
    hi = x.astype(BF16)
    lo = (x - hi.astype(F32)).astype(BF16)
    return hi, lo


def split3(x):
    hi = x.astype(BF16).astype(F32)
    mid = (x - hi).astype(BF16).astype(F32)
    return hi, mid, x - hi - mid


def total_of(x):
    return jnp.sum(jnp.sum(x, axis=0, keepdims=True), axis=1, keepdims=True)


def dot_nt(a, b):
    return lax.dot_general(a, b, (((1,), (1,)), ((), ())), preferred_element_type=F32)


def stacked_rows(rows, height, width):
    line = iota((height, width), 0)
    out = jnp.zeros((height, width), F32)
    for n, row in rows:
        out = jnp.where(line == n, row, out)
    return out


def columns_of(rows):
    wide = jnp.concatenate([rows, jnp.zeros((112, KB), F32)], axis=0)
    return jnp.transpose(wide)[:, 0:16]


def left_three(x):
    hi, lo = split2(x)
    return jnp.concatenate([hi, hi, lo], axis=1)


def right_three(x):
    hi, lo = split2(x)
    return jnp.concatenate([hi, lo, hi], axis=0)


def row_factor(row_ref):
    seg = row_ref[1:2, :]
    inside = seg == seg[:, 0:1]
    return inside, jnp.where(inside, jnp.exp2(LOG2E * row_ref[0:1, :]), 0.0)


def local_prefix(ld):
    upper = (iota((128, 128), 0) <= iota((128, 128), 1)).astype(F32)
    inside = dotx(jnp.concatenate([ld, jnp.zeros((6, 128), F32)], axis=0), upper)
    first = jnp.broadcast_to(inside[0:1, 127:128], (1, 128))
    second = jnp.broadcast_to(inside[1:2, 127:128], (1, 128))
    return (inside[0:1], inside[1:2] + first), first + second


def padded(src, dst):
    dst[0:144, :] = src[...]
    dst[144:256, :] = jnp.zeros((112, QR), BF16)


def own_columns(own_ref):
    cols = columns_of(jnp.concatenate([own_ref[...], jnp.zeros((8, KB), F32)], axis=0))
    return cols[:, 0:1], cols[:, 1:2]


def send_kernel(ld_ref, seg_ref, k_ref, bt_ref, out_ref, msg_ref):
    label = seg_ref[...].astype(F32)
    for k in range(NKEYS):
        out_ref[k, 0:2, :] = ld_ref[...]
        out_ref[k, 2:4, :] = label
    pre, total = local_prefix(ld_ref[...])
    msg_ref[0:KB, :] = k_ref[...]
    for h in range(2):
        rows = (*split3(total - pre[h]), label[h : h + 1], *split3(total), jnp.ones((1, 128), F32))
        msg_ref[KB + 64 * h : KB + 64 * (h + 1), :] = bt_ref[:, h * 128 : (h + 1) * 128]
        msg_ref[KB + 128 + 16 * h : KB + 144 + 16 * h, :] = stacked_rows(
            enumerate(rows), 16, 128
        ).astype(BF16)


def diag_kernel(x_ref, msg_ref, q_ref, row_ref, qaug_ref, kaug_ref, own_ref, st_ref, qaug):
    kk = lax.axis_index(KEYS)
    ld = jnp.concatenate([x_ref[a, 0:2, :] for a in range(NKEYS)], axis=0)
    sg = jnp.concatenate([x_ref[a, 2:4, :] for a in range(NKEYS)], axis=0)
    upper = (iota((128, 128), 0) <= iota((128, 128), 1)).astype(F32)
    within = dotx(ld, upper)
    tot = jnp.broadcast_to(within[:, 127:128], (16, 128))
    lower = (iota((16, 16), 1) < iota((16, 16), 0)).astype(F32)
    pre = within + dotx(lower, tot)
    row_ref[...] = jnp.zeros_like(row_ref)
    row_ref[0:1, :] = jnp.concatenate([pre[a : a + 1] for a in range(16)], axis=1)
    row_ref[1:2, :] = jnp.concatenate([sg[a : a + 1] for a in range(16)], axis=1)

    def own(arr):
        line = iota((16, 128), 0)
        halves = [
            jnp.sum(jnp.where(line == 2 * kk + h, arr, 0.0), axis=0, keepdims=True)
            for h in range(2)
        ]
        return jnp.concatenate(halves, axis=1)

    own_pre, own_seg = own(pre), own(sg)
    seg = row_ref[1:2, :]
    inside, _ = row_factor(row_ref)
    qaug_ref[0:128, :] = jnp.transpose(q_ref[...])
    doc_rows = [(10 + n, jnp.where(seg == float(n), 0.0, NEG)) for n in range(4)]
    qaug_ref[128:144, :] = stacked_rows(
        [(3, 1.0), (4, jnp.where(inside, 0.0, NEG)), *doc_rows], 16, QR
    ).astype(BF16)
    padded(qaug_ref, qaug)
    rows = list(enumerate(split3(own_pre * (-LOG2E / CS))))
    rows += [(7 + n, 1.0) for n in range(3)]
    rows += [(10 + n, jnp.where(own_seg == float(n), 1.0, 0.0)) for n in range(4)]
    cols = columns_of(stacked_rows(rows, 16, KB))
    kaug_ref[:, 0:128] = msg_ref[0:KB, :]
    kaug_ref[:, 128:256] = jnp.zeros((KB, 128), BF16)
    kaug_ref[:, 128:144] = cols.astype(BF16)
    own_ref[...] = stacked_rows([(0, own_pre), (1, own_seg)], 8, KB)
    st_ref[0:1, :] = jnp.full((1, QR), NEG, F32)
    st_ref[1:2, :] = jnp.ones((1, QR), F32)
    st_ref[2:8, :] = jnp.zeros((6, QR), F32)

    def chunk(q, carry):
        sl = pl.ds(pl.multiple_of(q * KB, KB), KB)
        causal = iota((KB, KB), 0) <= iota((KB, KB), 1) + (q - kk) * KB
        s = jnp.where(causal, dot(kaug_ref[...], qaug[:, sl]), NEG)
        top = jnp.max(s, axis=0, keepdims=True) * CS
        st_ref[0:1, sl] = top
        st_ref[1:2, sl] = jnp.sum(jnp.exp2(s * CS - top), axis=0, keepdims=True)
        return carry

    lax.fori_loop(kk, NKEYS, chunk, 0)


def slot_of(n, kk):
    return (n + 1 + kk) % 2


def shift_of(n, kk):
    return 2 * (n // 2) + 1 + kk % 2


def chunk_of(n, kk):
    return kk - kk % 2 + 1 - n % 2


def message(msgs, start, i, kk, doc):
    base = pl.multiple_of(slot_of(start + i, kk) * MSG, MSG)
    msg = msgs[i // 2].at[pl.ds(base, MSG)]
    meta = jnp.concatenate(
        [msg[KB + 128 : KB + 144, :], msg[KB + 144 : KB + 160, :]], axis=1
    ).astype(F32)
    bt = jnp.concatenate([msg[KB : KB + 64, :], msg[KB + 64 : KB + 128, :]], axis=1)
    seen = (meta[3:4] == doc) & (meta[7:8] > 0.0)
    here = LOG2E * (meta[0:1] + meta[1:2] + meta[2:3])
    total = meta[4:5, 0:128] + meta[5:6, 0:128] + meta[6:7, 0:128]
    return msg, bt, seen, here, jnp.where(seen, jnp.exp2(here), 0.0), total


def weighted(ahead, b, cols, row_ref, ct_ref, sl):
    causal = iota((KB, KB), 0) <= iota((KB, KB), 1) + ahead * KB
    seen = causal & (cols[1] == row_ref[1:2, sl])
    w = jnp.exp2(LOG2E * (row_ref[0:1, sl] - cols[0]))
    w = jnp.where(seen, w, 0.0)
    return seen, w * dot(b, ct_ref[:, sl]), w


def student_kernel(*refs):
    (btn_ref, btf_ref, vn_ref, vf_ref, qaug_ref, kaug_ref, own_ref, st_ref, row_ref, ct_ref, bt_ref,
     h_ref, dd_ref, gs_ref, qaug) = refs
    padded(qaug_ref, qaug)
    kk = lax.axis_index(KEYS)
    _, u = row_factor(row_ref)
    hi, lo = split2(ct_ref[...].astype(F32) * (u * u))
    h = dot_nt(hi, ct_ref[...]) + dot_nt(lo, ct_ref[...])
    h_ref[...] = h
    for n in range(BACK):
        bts, vs = (btn_ref, vn_ref) if n < HALF else (btf_ref, vf_ref)
        v = vs[n % HALF : n % HALF + 1, :]
        bv = bts[n % HALF].astype(F32) * v
        hi, lo = split2(bv)
        both = jnp.concatenate([hi, lo], axis=0)
        g = dot_nt(both, both)
        g = g[0:64, 0:64] + g[0:64, 64:128] + g[64:128, 0:64] + g[64:128, 64:128]
        gs_ref[n % HALF, :, (n // HALF) * 64 : (n // HALF) * 64 + 64] = g
    dd_ref[...] = jnp.zeros_like(dd_ref)
    cols = own_columns(own_ref)
    b = jnp.transpose(bt_ref[...].astype(F32)).astype(BF16)

    def chunk(q, carry):
        sl = pl.ds(pl.multiple_of(q * KB, KB), KB)
        seen, wi, _ = weighted(q - kk, b, cols, row_ref, ct_ref, sl)
        e = jnp.exp2(dot(kaug_ref[...], qaug[:, sl]) * CS - st_ref[0:1, sl])
        dd_ref[0:1, sl] = jnp.sum(jnp.where(seen, e, 0.0) * wi, axis=0, keepdims=True)
        dd_ref[1:2, sl] = jnp.sum(wi * wi, axis=0, keepdims=True)
        return carry

    lax.fori_loop(kk, NKEYS, chunk, 0)


def tiles_in(row_ref):
    seg = row_ref[1:2, :]
    count = jnp.sum(jnp.where(seg == seg[:, 0:1], 1.0, 0.0))
    return (count.astype(jnp.int32) + (TQ - 1)) // TQ


def after(pos, many, tiles, empty):
    n, t = pos
    wrap = t + 1 >= tiles
    n = jnp.where(wrap, n + 1, n)
    return jnp.where(n >= many, empty, n), jnp.where(wrap, 0, t + 1)


def lanes(pos):
    return pl.ds(pl.multiple_of(pos[1] * TQ, TQ), TQ)


def totals_of(start, stop, msgs, refs, outs, scratch):
    qaug, ct_ref, row_ref = refs
    mref_ref, d_ref, kaug, bts_ref, nb_ref, sum_ref, v_ref = outs
    bl, cc, m_acc, l_acc, s_a, s_b, i_a, i_b, qpad = scratch
    padded(qaug, qpad)
    kk = lax.axis_index(KEYS)
    doc = row_ref[1:2, 0:1]
    mref_ref[...] = jnp.full_like(mref_ref, NEG)
    d_ref[...] = jnp.zeros_like(d_ref)
    cc[0:64, :] = ct_ref[...]
    cc[64:128, :] = ct_ref[...]
    lane = iota((KB, 128), 1)
    empty = stop - start
    kaug[empty, :, 0:128] = jnp.zeros((KB, 128), BF16)
    kaug[empty, :, 128:256] = jnp.where((lane == 0) | (lane == 3), NEG, 0.0).astype(BF16)
    bts_ref[empty] = jnp.zeros((STATE, KB), BF16)
    bl[empty] = jnp.zeros((KB, 128), BF16)
    count = jnp.int32(0)
    lane1 = iota((1, 128), 1)
    totals = jnp.zeros((1, 128), F32)
    for i in range(stop - start):
        msg, bt, seen, here, v, total = message(msgs, start, i, kk, doc)
        totals = jnp.where(lane1 == start + i, total, totals)
        active = jnp.max(jnp.where(seen, 1.0, 0.0)) > 0.0
        count = count + active.astype(jnp.int32)
        rows = list(enumerate(split3(jnp.where(seen, here * (1.0 / CS), NEG))))
        rows += [(3, jnp.where(seen, 0.0, NEG)), (4, 1.0), (5, 1.0), (6, 1.0)]
        kaug[i, :, 0:128] = msg[0:KB, :]
        kaug[i, :, 128:256] = jnp.zeros((KB, 128), BF16)
        kaug[i, :, 128:144] = columns_of(stacked_rows(rows, 16, KB)).astype(BF16)
        bts_ref[i] = bt
        v_ref[i : i + 1, :] = v
        bv = bt.astype(F32) * v
        hi = bv.astype(BF16).astype(F32)
        bl[i] = jnp.transpose(jnp.concatenate([hi, bv - hi], axis=0)).astype(BF16)

    nb_ref[0] = count
    sum_ref[...] = jnp.broadcast_to(totals, (8, 128))
    tiles = tiles_in(row_ref)

    def scores(pos, s_buf, i_buf):
        s_buf[...] = dot(kaug[pos[0]], qpad[:, lanes(pos)])
        i_buf[...] = dot(bl[pos[0]], cc[:, lanes(pos)])

    def work(pos, s_buf, i_buf):
        sl = lanes(pos)
        old = m_acc[:, sl]
        new = jnp.maximum(old, jnp.max(s_buf[...], axis=0, keepdims=True) * CS)
        e = jnp.exp2(s_buf[...] * CS - new)
        l_acc[:, sl] = l_acc[:, sl] * jnp.exp2(old - new) + jnp.sum(e, axis=0, keepdims=True)
        m_acc[:, sl] = new
        mref_ref[pl.ds(pos[0], 1), sl] = new
        d_ref[pl.ds(pos[0], 1), sl] = jnp.sum(e * i_buf[...], axis=0, keepdims=True)

    @pl.when(count > 0)
    def _():
        first = (jnp.int32(0), jnp.int32(0))
        scores(first, s_a, i_a)

        def step(_, pos):
            second = after(pos, count, tiles, empty)
            third = after(second, count, tiles, empty)
            scores(second, s_b, i_b)
            work(pos, s_a, i_a)
            scores(third, s_a, i_a)
            work(second, s_b, i_b)
            return third

        lax.fori_loop(0, (count * tiles + 1) // 2, step, first)


def stats_far_kernel(m0, m1, qaug, ct_ref, row_ref, st_ref, *rest):
    outs, ml_ref, scratch = rest[:7], rest[7], rest[8:]
    scratch[2][...] = st_ref[0:1, :]
    scratch[3][...] = st_ref[1:2, :]
    totals_of(HALF, BACK, (m0, m1), (qaug, ct_ref, row_ref), outs, scratch)
    ml_ref[0:1, :] = scratch[2][...]
    ml_ref[1:2, :] = scratch[3][...]


def stats_near_kernel(m0, m1, qaug, ct_ref, row_ref, ml_ref, far_ref, *rest):
    outs, send_ref, scratch = rest[:7], rest[7], rest[8:]
    scratch[2][...] = ml_ref[0:1, :]
    scratch[3][...] = ml_ref[1:2, :]
    totals_of(0, HALF, (m0, m1), (qaug, ct_ref, row_ref), outs, scratch)
    lse = scratch[2][...] + jnp.log2(scratch[3][...])
    totals = outs[5][0:1, :] + far_ref[0:1, :]
    for k in range(NKEYS):
        send_ref[k, 0:1, :] = lse
        send_ref[k, 1:2, 0:128] = totals


def scale_kernel(recv_ref, st_ref, dd_ref, row_ref, ct_ref, mn_ref, mf_ref, dn_ref, df_ref,
                 gs_ref, h_ref, scal_ref, aug_ref, os_ref, eo_ref):
    kk = lax.axis_index(KEYS)
    parts = [recv_ref[k, 0:1, :] for k in range(NKEYS)]
    top = functools.reduce(jnp.maximum, parts)
    lse = top + jnp.log2(sum(jnp.exp2(p - top) for p in parts))
    totals = jnp.concatenate([recv_ref[k, 1:2, 0:128] for k in range(NKEYS)], axis=0)
    dev, lane = iota((NKEYS, 128), 0), iota((NKEYS, 128), 1)
    away = 8 * shift_of(lane, dev) - chunk_of(lane, dev)
    offs = []
    for n in range(BACK):
        nearer = (lane < BACK) & (away < 8 * shift_of(n, kk) - chunk_of(n, kk))
        off = total_of(jnp.where(nearer, totals, 0.0))
        offs.append((n, jnp.broadcast_to(off, (1, 128))))
    eo = jnp.exp2(LOG2E * stacked_rows(offs, 8, 128))
    eo_ref[0:8, :] = jnp.concatenate([eo] * 4, axis=1)
    eo_ref[8:16, :] = jnp.zeros((8, TQ), F32)
    seg = row_ref[1:2, :]
    inside, u = row_factor(row_ref)
    beta = (LOG2E * row_ref[0:1, :] - lse) * (1.0 / CS)
    rows = [(n, 1.0) for n in range(3)]
    rows += [(4 + n, part) for n, part in enumerate(split3(jnp.where(inside, beta, NEG)))]
    rows += [(7 + n, part) for n, part in enumerate(split3(beta))]
    rows += [(10 + n, jnp.where(seg == float(n), 0.0, NEG)) for n in range(4)]
    aug_ref[...] = stacked_rows(rows, 16, QR).astype(BF16)
    ctf = ct_ref[...].astype(F32)
    h = h_ref[...]
    g_all = jnp.zeros((STATE, STATE), F32)
    ast = []
    for n in range(BACK):
        weighted = gs_ref[n % HALF, :, (n // HALF) * 64 : (n // HALF) * 64 + 64] * (eo[n : n + 1, 0:64] * eo[n : n + 1, 0:64])
        g_all = g_all + weighted
        ast.append(total_of(weighted * h) * (2.0 / SEQ))
    os = dot(left_three(g_all * (2.0 / SEQ)), right_three(ctf * (u * u)))
    os_ref[...] = os
    near = dd_ref[1:2, :] * (2.0 / SEQ) - 2.0 * jnp.exp2(st_ref[0:1, :] - lse) * dd_ref[0:1, :]
    mref = jnp.concatenate([mn_ref[0:HALF, :], mf_ref[0:HALF, :]], axis=0)
    d = jnp.concatenate([dn_ref[0:HALF, :], df_ref[0:HALF, :]], axis=0)
    far = jnp.where(inside, jnp.exp2(mref - lse) * u * d, 0.0)
    far = -2.0 * eo[:, 0:1] * far
    along = near + jnp.sum(ctf * os, axis=0, keepdims=True) + jnp.sum(far, axis=0, keepdims=True)
    far = jnp.sum(far, axis=1, keepdims=True)
    lane = iota((1, 128), 1)
    out = jnp.where(lane == 0, total_of(near), 0.0)
    for n in range(BACK):
        out = jnp.where(lane == n + 1, far[n : n + 1, :] + ast[n], out)
    for q in range(NKEYS):
        part = jnp.sum(along[:, q * KB : (q + 1) * KB], axis=1, keepdims=True)
        out = jnp.where(lane == 16 + q, part, out)
    scal_ref[...] = jnp.broadcast_to(out, (8, 128))


def gradients(start, stop, refs, outs, o_acc, scratch):
    nb_ref, kaug, bts, h_ref, v_ref, qaug_ref, aug_ref, ct_ref, row_ref, eo_ref = refs
    qaug, g_acc, s_a, s_b, h_a, h_b, l_a, l_b = scratch
    kk = lax.axis_index(KEYS)
    padded(qaug_ref, qaug)
    qaug[128:144, :] = aug_ref[...]
    g_acc[...] = jnp.zeros_like(g_acc)
    count = nb_ref[0]
    empty = stop - start
    tiles = tiles_in(row_ref)

    def scores(pos, s_buf):
        s_buf[...] = dot(kaug[pos[0]], qaug[:, lanes(pos)])

    def weigh(s_buf, h_buf, l_buf):
        hi, lo = split2(jnp.exp2(CS * s_buf[...]))
        h_buf[...] = hi
        l_buf[...] = lo

    def add(pos, h_buf, l_buf):
        sl = lanes(pos)
        c, b = ct_ref[:, sl], bts[pos[0]]
        g = dot_nt(c, h_buf[...]) + dot_nt(c, l_buf[...])
        g_acc[pl.ds(pos[0], 1)] += g.reshape(1, STATE, KB)
        o = dot(b, h_buf[...]) + dot(b, l_buf[...])
        o_acc[:, sl] += o * eo_ref[pl.ds(pos[0] + start, 1), :]

    @pl.when(count > 0)
    def _():
        first = (jnp.int32(0), jnp.int32(0))
        scores(first, s_a)
        weigh(s_a, h_a, l_a)
        second = after(first, count, tiles, empty)
        scores(second, s_b)

        def step(_, carry):
            pos, second = carry[:2], carry[2:]
            third = after(second, count, tiles, empty)
            fourth = after(third, count, tiles, empty)
            add(pos, h_a, l_a)
            weigh(s_b, h_b, l_b)
            scores(third, s_a)
            add(second, h_b, l_b)
            weigh(s_a, h_a, l_a)
            scores(fourth, s_b)
            return (*third, *fourth)

        lax.fori_loop(0, (count * tiles + 1) // 2, step, (*first, *second))

    h_left = left_three(h_ref[...])
    for n in range(start, stop):
        e = eo_ref[n : n + 1, 0:KB]
        v = v_ref[n - start : n - start + 1, :] * e
        student = dot(h_left, right_three(bts[n - start].astype(F32) * v)) * v
        out = pl.ds(pl.multiple_of(slot_of(n, kk) * STATE, STATE), STATE)
        outs[(n - start) // 2][out, :] = (2.0 / SEQ) * student - 2.0 * e * g_acc[n - start]


def far_kernel(*refs):
    o_ref = refs[12]
    o_ref[...] = jnp.zeros_like(o_ref)
    gradients(HALF, BACK, refs[:10], refs[10:12], o_ref, refs[13:])


def near_kernel(*refs):
    os_ref, kd_ref, btd_ref, own_ref, o_ref, scal_ref = refs[10:16]
    gb_ref, gc_ref, o_acc, *scratch = refs[18:]
    o_acc[...] = o_ref[...]
    gradients(0, HALF, refs[:10], refs[16:18], o_acc, scratch)
    qaug, ct_ref, row_ref = scratch[0], refs[7], refs[8]
    kk = lax.axis_index(KEYS)
    gb_ref[...] = jnp.zeros_like(gb_ref)
    bt = btd_ref[...]
    cols = own_columns(own_ref)
    b = jnp.transpose(bt.astype(F32)).astype(BF16)

    def chunk(q, carry):
        sl = pl.ds(pl.multiple_of(q * KB, KB), KB)
        seen, wi, w = weighted(q - kk, b, cols, row_ref, ct_ref, sl)
        p = jnp.where(seen, jnp.exp2(CS * dot(kd_ref[...], qaug[:, sl])), 0.0)
        hi, lo = split2(p - w * wi * (1.0 / SEQ))
        c = ct_ref[:, sl]
        gb_ref[...] -= 2.0 * (dot_nt(c, hi) + dot_nt(c, lo))
        o_acc[:, sl] += dot(bt, hi) + dot(bt, lo)
        return carry

    lax.fori_loop(kk, NKEYS, chunk, 0)
    for k in range(NKEYS):
        sl = slice(k * KB, (k + 1) * KB)
        gc_ref[k, 0:STATE, :] = os_ref[:, sl] - 2.0 * o_acc[:, sl]
        gc_ref[k, STATE : STATE + 8, 0:128] = scal_ref[...]


def final_kernel(*refs):
    got = refs[:HOPS]
    swap_ref, gb_ref, gc_ref, scal_ref, bt_ref, ct_ref, out_c, out_b, out_d = refs[HOPS:]
    row, kk = lax.axis_index(ROWS), lax.axis_index(KEYS)
    gb = functools.reduce(jnp.add, [g[0:STATE, :] for g in got]) + gb_ref[...] + swap_ref[...]
    gc = functools.reduce(jnp.add, [gc_ref[k, 0:STATE, :] for k in range(NKEYS)])
    out_b[...] = gb
    out_c[...] = gc
    c = ct_ref[:, pl.ds(pl.multiple_of(kk * KB, KB), KB)].astype(F32)
    lead = jnp.sum(c * gc - bt_ref[...].astype(F32) * gb, axis=0, keepdims=True)
    later = (iota((KB, KB), 0) >= iota((KB, KB), 1)).astype(F32)
    local = dotx(jnp.broadcast_to(lead, (8, KB)), later)
    me = row * NKEYS + kk
    dev, lane = iota((128, 128), 0), iota((128, 128), 1)
    at, block = dev % NKEYS, lane - 1
    first = dev - at
    chunk = first - NKEYS * shift_of(block, at) + chunk_of(block, at)
    chunk = jnp.where(lane >= 16, first + lane - 16, jnp.where(lane == 0, dev, chunk))
    sign = jnp.where(lane <= BACK, -1.0, jnp.where((lane >= 16) & (lane < 24), 1.0, 0.0))
    tail = total_of(jnp.where(chunk > me, sign * scal_ref[...], 0.0))
    out_d[...] = (local[0:1, :] + tail) * (1.0 / SEQ)


def call(kernel, **how):
    params = pltpu.CompilerParams(vmem_limit_bytes=20 * 1024 * 1024)
    return pl.pallas_call(kernel, compiler_params=params, **how)


def sds(shape, dtype=F32):
    return jax.ShapeDtypeStruct(shape, dtype)


def vmem():
    return pl.BlockSpec(memory_space=pltpu.VMEM)


def smem():
    return pl.BlockSpec(memory_space=pltpu.SMEM)


PAIRS = [(k, k ^ 1) for k in range(NKEYS)]
HOP_PAIRS = [
    [
        (r * NKEYS + k, (r + shift_of(2 * j, k)) * NKEYS + k)
        for r in range(NROWS)
        for k in range(NKEYS)
        if r + shift_of(2 * j, k) < NROWS
    ]
    for j in range(HOPS)
]


def on_device(queries, keys_in, c_proj, b_proj, log_decay, segments):
    ct, bt = c_proj.T, b_proj.T
    x, msg = pl.pallas_call(
        send_kernel, out_shape=(sds((NKEYS, 4, 128)), sds((MSG, 128), BF16)), name="send"
    )(log_decay.reshape(2, 128), segments.reshape(2, 128), keys_in, bt)
    x = lax.all_to_all(x, KEYS, 0, 0, tiled=True)
    other = lax.ppermute(msg, KEYS, PAIRS)
    pair = jnp.concatenate([msg, other], axis=0)
    msgs = [lax.ppermute(pair, BOTH, hop) for hop in HOP_PAIRS]
    rowmeta, qaug, kd, own, st = call(
        diag_kernel,
        out_shape=(
            sds((8, QR)), sds((144, QR), BF16), sds((KB, 256), BF16), sds((8, KB)),
            sds((8, QR)),
        ),
        scratch_shapes=[pltpu.VMEM((256, QR), BF16)],
        name="diag",
    )(x, msg, queries)

    def stats(kernel, last, name):
        return call(
            kernel,
            out_shape=(
                sds((8, QR)), sds((8, QR)), sds((HALF + 1, KB, 256), BF16),
                sds((HALF + 1, STATE, KB), BF16), sds((1,), jnp.int32), sds((8, 128)),
                sds((8, KB)), last,
            ),
            out_specs=(*[vmem()] * 4, smem(), *[vmem()] * 3),
            scratch_shapes=[
                pltpu.VMEM((HALF + 1, KB, 128), BF16), pltpu.VMEM((128, QR), BF16),
                pltpu.VMEM((1, QR), F32), pltpu.VMEM((1, QR), F32),
                *[pltpu.VMEM((KB, TQ), F32)] * 4, pltpu.VMEM((256, QR), BF16),
            ],
            name=name,
        )

    mf, df, *parts_far, sums, vf, ml = stats(stats_far_kernel, sds((8, QR)), "statsfar")(
        *msgs[2:], qaug, ct, rowmeta, st
    )
    mn, dn, *parts_near, _, vn, send = stats(stats_near_kernel, sds((NKEYS, 2, QR)), "statsnear")(
        *msgs[:2], qaug, ct, rowmeta, ml, sums
    )
    recv = lax.all_to_all(send, KEYS, 0, 0, tiled=True)
    h, dd, gs = call(
        student_kernel,
        out_shape=(
            sds((STATE, STATE)), sds((8, QR)),
            sds((HALF, STATE, 2 * STATE)),
        ),
        scratch_shapes=[pltpu.VMEM((256, QR), BF16)],
        name="student",
    )(parts_near[1], parts_far[1], vn, vf, qaug, kd, own, st, rowmeta, ct, bt)
    scal, aug, os, eo = call(
        scale_kernel,
        out_shape=(
            sds((8, 128)), sds((16, QR), BF16), sds((STATE, QR)), sds((16, TQ)),
        ),
        name="scale",
    )(recv, st, dd, rowmeta, ct, mn, mf, dn, df, gs, h)

    def shared(parts, v):
        kaug, bts, nb = parts
        return nb, kaug, bts, h, v, qaug, aug, ct, rowmeta, eo

    scratch = [
        pltpu.VMEM((256, QR), BF16), pltpu.VMEM((HALF + 1, STATE, KB), F32),
        *[pltpu.VMEM((KB, TQ), F32)] * 2, *[pltpu.VMEM((KB, TQ), BF16)] * 4,
    ]
    *far, o = call(
        far_kernel,
        in_specs=[smem(), *[vmem()] * 9],
        out_shape=(*[sds((2 * STATE, KB))] * 2, sds((STATE, QR))),
        scratch_shapes=scratch,
        name="far",
    )(*shared(parts_far, vf))
    back = [lax.ppermute(g, BOTH, [(b, a) for a, b in hop]) for g, hop in zip(far, HOP_PAIRS[2:])]
    *near, gb, gc = call(
        near_kernel,
        in_specs=[smem(), *[vmem()] * 15],
        out_shape=(*[sds((2 * STATE, KB))] * 2, sds((STATE, KB)), sds((NKEYS, STATE + 8, KB))),
        scratch_shapes=[pltpu.VMEM((STATE, QR), F32), *scratch],
        name="near",
    )(*shared(parts_near, vn), os, kd, bt, own, o, scal)
    gc = lax.all_to_all(gc, KEYS, 0, 0, tiled=True)
    scal = jnp.broadcast_to(gc[:, STATE, 0:128], (NROWS, NKEYS, 128))
    scal = lax.all_to_all(scal, ROWS, 0, 0, tiled=True).reshape(NROWS * NKEYS, 128)
    back += [lax.ppermute(g, BOTH, [(b, a) for a, b in hop]) for g, hop in zip(near, HOP_PAIRS)]
    other = functools.reduce(jnp.add, [g[STATE:, :] for g in back])
    other = lax.ppermute(other, KEYS, PAIRS)
    out_c, out_b, out_d = call(
        final_kernel,
        out_shape=(sds((STATE, KB)), sds((STATE, KB)), sds((1, KB))),
        name="final",
    )(*back, other, gb, gc, scal, bt, ct)
    return out_c.T, out_b.T, out_d.reshape(KB)


def solution(mesh):
    return jax.shard_map(
        on_device,
        mesh=mesh,
        in_specs=(
            P(ROWS, None), P(BOTH, None), P(ROWS, None), P(BOTH, None), P(BOTH), P(BOTH),
        ),
        out_specs=(P(BOTH, None), P(BOTH, None), P(BOTH)),
        check_vma=False,
    )
```

```python
import functools

import jax
import jax.numpy as jnp
from jax import lax
from jax.experimental import pallas as pl
from jax.experimental.pallas import tpu as pltpu
from jax.sharding import PartitionSpec as P


ROWS = "rows"
KEYS = "keys"
BOTH = ("rows", "keys")
BACK = 8
HALF = BACK // 2
NROWS = 16
NKEYS = 8
KB = 256
QR = KB * NKEYS
HEAD = 128
STATE = 64
SEQ = QR * NROWS
LOG2E = 1.4426950408889634
CS = HEAD**-0.5 * LOG2E
NEG = -1e30
TQ = 512
MSG = KB + 128 + 32
F32 = jnp.float32
BF16 = jnp.bfloat16
HI = lax.Precision.HIGHEST


def dot(a, b):
    return jnp.dot(a, b, preferred_element_type=F32)


def dotx(a, b):
    return jnp.dot(a, b, precision=HI, preferred_element_type=F32)


def iota(shape, dim):
    return lax.broadcasted_iota(jnp.int32, shape, dim)


def split2(x):
    hi = x.astype(BF16)
    lo = (x - hi.astype(F32)).astype(BF16)
    return hi, lo


def split3(x):
    hi = x.astype(BF16).astype(F32)
    mid = (x - hi).astype(BF16).astype(F32)
    return hi, mid, x - hi - mid


def total_of(x):
    return jnp.sum(jnp.sum(x, axis=0, keepdims=True), axis=1, keepdims=True)


def dot_nt(a, b):
    return lax.dot_general(a, b, (((1,), (1,)), ((), ())), preferred_element_type=F32)


def stacked_rows(rows, height, width):
    line = iota((height, width), 0)
    out = jnp.zeros((height, width), F32)
    for n, row in rows:
        out = jnp.where(line == n, row, out)
    return out


def columns_of(rows):
    wide = jnp.concatenate([rows, jnp.zeros((112, KB), F32)], axis=0)
    return jnp.transpose(wide)[:, 0:16]


def left_three(x):
    hi, lo = split2(x)
    return jnp.concatenate([hi, hi, lo], axis=1)


def right_three(x):
    hi, lo = split2(x)
    return jnp.concatenate([hi, lo, hi], axis=0)


def row_factor(row_ref):
    seg = row_ref[1:2, :]
    inside = seg == seg[:, 0:1]
    return inside, jnp.where(inside, jnp.exp2(LOG2E * row_ref[0:1, :]), 0.0)


def local_prefix(ld):
    upper = (iota((128, 128), 0) <= iota((128, 128), 1)).astype(F32)
    inside = dotx(jnp.concatenate([ld, jnp.zeros((6, 128), F32)], axis=0), upper)
    first = jnp.broadcast_to(inside[0:1, 127:128], (1, 128))
    second = jnp.broadcast_to(inside[1:2, 127:128], (1, 128))
    return (inside[0:1], inside[1:2] + first), first + second


def padded(src, dst):
    dst[0:144, :] = src[...]
    dst[144:256, :] = jnp.zeros((112, QR), BF16)


def own_columns(own_ref):
    cols = columns_of(jnp.concatenate([own_ref[...], jnp.zeros((8, KB), F32)], axis=0))
    return cols[:, 0:1], cols[:, 1:2]


def send_kernel(ld_ref, seg_ref, k_ref, bt_ref, out_ref, msg_ref, pair_ref):
    label = seg_ref[...].astype(F32)
    for k in range(NKEYS):
        out_ref[k, 0:2, :] = ld_ref[...]
        out_ref[k, 2:4, :] = label
    pre, total = local_prefix(ld_ref[...])
    msg_ref[0:KB, :] = k_ref[...]
    for h in range(2):
        rows = (*split3(total - pre[h]), label[h : h + 1], *split3(total), jnp.ones((1, 128), F32))
        msg_ref[KB + 64 * h : KB + 64 * (h + 1), :] = bt_ref[:, h * 128 : (h + 1) * 128]
        msg_ref[KB + 128 + 16 * h : KB + 144 + 16 * h, :] = stacked_rows(
            enumerate(rows), 16, 128
        ).astype(BF16)
    pair_ref[0:MSG, :] = msg_ref[...]
    pair_ref[MSG:, :] = jnp.zeros((MSG, 128), BF16)


def diag_kernel(x_ref, msg_ref, q_ref, row_ref, qaug_ref, kaug_ref, own_ref, st_ref, qaug):
    kk = lax.axis_index(KEYS)
    ld = jnp.concatenate([x_ref[a, 0:2, :] for a in range(NKEYS)], axis=0)
    sg = jnp.concatenate([x_ref[a, 2:4, :] for a in range(NKEYS)], axis=0)
    upper = (iota((128, 128), 0) <= iota((128, 128), 1)).astype(F32)
    within = dotx(ld, upper)
    tot = jnp.broadcast_to(within[:, 127:128], (16, 128))
    lower = (iota((16, 16), 1) < iota((16, 16), 0)).astype(F32)
    pre = within + dotx(lower, tot)
    row_ref[...] = jnp.zeros_like(row_ref)
    row_ref[0:1, :] = jnp.concatenate([pre[a : a + 1] for a in range(16)], axis=1)
    row_ref[1:2, :] = jnp.concatenate([sg[a : a + 1] for a in range(16)], axis=1)

    def own(arr):
        line = iota((16, 128), 0)
        halves = [
            jnp.sum(jnp.where(line == 2 * kk + h, arr, 0.0), axis=0, keepdims=True)
            for h in range(2)
        ]
        return jnp.concatenate(halves, axis=1)

    own_pre, own_seg = own(pre), own(sg)
    seg = row_ref[1:2, :]
    inside, _ = row_factor(row_ref)
    qaug_ref[0:128, :] = jnp.transpose(q_ref[...])
    doc_rows = [(10 + n, jnp.where(seg == float(n), 0.0, NEG)) for n in range(4)]
    qaug_ref[128:144, :] = stacked_rows(
        [(3, 1.0), (4, jnp.where(inside, 0.0, NEG)), *doc_rows], 16, QR
    ).astype(BF16)
    padded(qaug_ref, qaug)
    rows = list(enumerate(split3(own_pre * (-LOG2E / CS))))
    rows += [(7 + n, 1.0) for n in range(3)]
    rows += [(10 + n, jnp.where(own_seg == float(n), 1.0, 0.0)) for n in range(4)]
    cols = columns_of(stacked_rows(rows, 16, KB))
    kaug_ref[:, 0:128] = msg_ref[0:KB, :]
    kaug_ref[:, 128:256] = jnp.zeros((KB, 128), BF16)
    kaug_ref[:, 128:144] = cols.astype(BF16)
    own_ref[...] = stacked_rows([(0, own_pre), (1, own_seg)], 8, KB)
    st_ref[0:1, :] = jnp.full((1, QR), NEG, F32)
    st_ref[1:2, :] = jnp.ones((1, QR), F32)
    st_ref[2:8, :] = jnp.zeros((6, QR), F32)

    def chunk(q, carry):
        sl = pl.ds(pl.multiple_of(q * KB, KB), KB)
        causal = iota((KB, KB), 0) <= iota((KB, KB), 1) + (q - kk) * KB
        s = jnp.where(causal, dot(kaug_ref[...], qaug[:, sl]), NEG)
        top = jnp.max(s, axis=0, keepdims=True) * CS
        st_ref[0:1, sl] = top
        st_ref[1:2, sl] = jnp.sum(jnp.exp2(s * CS - top), axis=0, keepdims=True)
        return carry

    lax.fori_loop(kk, NKEYS, chunk, 0)


def slot_of(n, kk):
    return (n + 1 + kk) % 2


def shift_of(n, kk):
    return 2 * (n // 2) + 1 + kk % 2


def chunk_of(n, kk):
    return kk - kk % 2 + 1 - n % 2


def message(msgs, start, i, kk, doc):
    base = pl.multiple_of(slot_of(start + i, kk) * MSG, MSG)
    msg = msgs[i // 2].at[pl.ds(base, MSG)]
    meta = jnp.concatenate(
        [msg[KB + 128 : KB + 144, :], msg[KB + 144 : KB + 160, :]], axis=1
    ).astype(F32)
    bt = jnp.concatenate([msg[KB : KB + 64, :], msg[KB + 64 : KB + 128, :]], axis=1)
    seen = (meta[3:4] == doc) & (meta[7:8] > 0.0)
    here = LOG2E * (meta[0:1] + meta[1:2] + meta[2:3])
    total = meta[4:5, 0:128] + meta[5:6, 0:128] + meta[6:7, 0:128]
    return msg, bt, seen, here, jnp.where(seen, jnp.exp2(here), 0.0), total


def weighted(ahead, b, cols, row_ref, ct_ref, sl):
    causal = iota((KB, KB), 0) <= iota((KB, KB), 1) + ahead * KB
    seen = causal & (cols[1] == row_ref[1:2, sl])
    w = jnp.exp2(LOG2E * (row_ref[0:1, sl] - cols[0]))
    w = jnp.where(seen, w, 0.0)
    return seen, w * dot(b, ct_ref[:, sl]), w


def student_kernel(*refs):
    (btn_ref, btf_ref, vn_ref, vf_ref, qaug_ref, kaug_ref, own_ref, st_ref, row_ref, ct_ref, bt_ref,
     h_ref, dd_ref, gs_ref, qaug) = refs
    padded(qaug_ref, qaug)
    kk = lax.axis_index(KEYS)
    _, u = row_factor(row_ref)
    hi, lo = split2(ct_ref[...].astype(F32) * (u * u))
    h = dot_nt(hi, ct_ref[...]) + dot_nt(lo, ct_ref[...])
    h_ref[...] = h
    for n in range(BACK):
        bts, vs = (btn_ref, vn_ref) if n < HALF else (btf_ref, vf_ref)
        v = vs[n % HALF : n % HALF + 1, :]
        bv = bts[n % HALF].astype(F32) * v
        hi, lo = split2(bv)
        both = jnp.concatenate([hi, lo], axis=0)
        g = dot_nt(both, both)
        g = g[0:64, 0:64] + g[0:64, 64:128] + g[64:128, 0:64] + g[64:128, 64:128]
        gs_ref[n % HALF, :, (n // HALF) * 64 : (n // HALF) * 64 + 64] = g
    dd_ref[...] = jnp.zeros_like(dd_ref)
    cols = own_columns(own_ref)
    b = jnp.transpose(bt_ref[...].astype(F32)).astype(BF16)

    def chunk(q, carry):
        sl = pl.ds(pl.multiple_of(q * KB, KB), KB)
        seen, wi, _ = weighted(q - kk, b, cols, row_ref, ct_ref, sl)
        e = jnp.exp2(dot(kaug_ref[...], qaug[:, sl]) * CS - st_ref[0:1, sl])
        dd_ref[0:1, sl] = jnp.sum(jnp.where(seen, e, 0.0) * wi, axis=0, keepdims=True)
        dd_ref[1:2, sl] = jnp.sum(wi * wi, axis=0, keepdims=True)
        return carry

    lax.fori_loop(kk, NKEYS, chunk, 0)


def tiles_in(row_ref):
    seg = row_ref[1:2, :]
    count = jnp.sum(jnp.where(seg == seg[:, 0:1], 1.0, 0.0))
    return (count.astype(jnp.int32) + (TQ - 1)) // TQ


def after(pos, many, tiles, empty):
    n, t = pos
    wrap = t + 1 >= tiles
    n = jnp.where(wrap, n + 1, n)
    return jnp.where(n >= many, empty, n), jnp.where(wrap, 0, t + 1)


def lanes(pos):
    return pl.ds(pl.multiple_of(pos[1] * TQ, TQ), TQ)


def totals_of(start, stop, msgs, refs, outs, scratch):
    qaug, ct_ref, row_ref = refs
    mref_ref, d_ref, kaug, bts_ref, nb_ref, sum_ref, v_ref = outs
    bl, cc, m_acc, l_acc, s_a, s_b, i_a, i_b, qpad = scratch
    padded(qaug, qpad)
    kk = lax.axis_index(KEYS)
    doc = row_ref[1:2, 0:1]
    mref_ref[...] = jnp.full_like(mref_ref, NEG)
    d_ref[...] = jnp.zeros_like(d_ref)
    cc[0:64, :] = ct_ref[...]
    cc[64:128, :] = ct_ref[...]
    lane = iota((KB, 128), 1)
    empty = stop - start
    kaug[empty, :, 0:128] = jnp.zeros((KB, 128), BF16)
    kaug[empty, :, 128:256] = jnp.where((lane == 0) | (lane == 3), NEG, 0.0).astype(BF16)
    bts_ref[empty] = jnp.zeros((STATE, KB), BF16)
    bl[empty] = jnp.zeros((KB, 128), BF16)
    count = jnp.int32(0)
    lane1 = iota((1, 128), 1)
    totals = jnp.zeros((1, 128), F32)
    for i in range(stop - start):
        msg, bt, seen, here, v, total = message(msgs, start, i, kk, doc)
        totals = jnp.where(lane1 == start + i, total, totals)
        active = jnp.max(jnp.where(seen, 1.0, 0.0)) > 0.0
        count = count + active.astype(jnp.int32)
        rows = list(enumerate(split3(jnp.where(seen, here * (1.0 / CS), NEG))))
        rows += [(3, jnp.where(seen, 0.0, NEG)), (4, 1.0), (5, 1.0), (6, 1.0)]
        kaug[i, :, 0:128] = msg[0:KB, :]
        kaug[i, :, 128:256] = jnp.zeros((KB, 128), BF16)
        kaug[i, :, 128:144] = columns_of(stacked_rows(rows, 16, KB)).astype(BF16)
        bts_ref[i] = bt
        v_ref[i : i + 1, :] = v
        bv = bt.astype(F32) * v
        hi = bv.astype(BF16).astype(F32)
        bl[i] = jnp.transpose(jnp.concatenate([hi, bv - hi], axis=0)).astype(BF16)

    nb_ref[0] = count
    sum_ref[...] = jnp.broadcast_to(totals, (8, 128))
    tiles = tiles_in(row_ref)

    def scores(pos, s_buf, i_buf):
        s_buf[...] = dot(kaug[pos[0]], qpad[:, lanes(pos)])
        i_buf[...] = dot(bl[pos[0]], cc[:, lanes(pos)])

    def work(pos, s_buf, i_buf):
        sl = lanes(pos)
        old = m_acc[:, sl]
        new = jnp.maximum(old, jnp.max(s_buf[...], axis=0, keepdims=True) * CS)
        e = jnp.exp2(s_buf[...] * CS - new)
        l_acc[:, sl] = l_acc[:, sl] * jnp.exp2(old - new) + jnp.sum(e, axis=0, keepdims=True)
        m_acc[:, sl] = new
        mref_ref[pl.ds(pos[0], 1), sl] = new
        d_ref[pl.ds(pos[0], 1), sl] = jnp.sum(e * i_buf[...], axis=0, keepdims=True)

    @pl.when(count > 0)
    def _():
        first = (jnp.int32(0), jnp.int32(0))
        scores(first, s_a, i_a)

        def step(_, pos):
            second = after(pos, count, tiles, empty)
            third = after(second, count, tiles, empty)
            scores(second, s_b, i_b)
            work(pos, s_a, i_a)
            scores(third, s_a, i_a)
            work(second, s_b, i_b)
            return third

        lax.fori_loop(0, (count * tiles + 1) // 2, step, first)


def stats_near_kernel(m0, m1, qaug, ct_ref, row_ref, st_ref, *rest):
    outs, ml_ref, scratch = rest[:7], rest[7], rest[8:]
    scratch[2][...] = st_ref[0:1, :]
    scratch[3][...] = st_ref[1:2, :]
    totals_of(0, HALF, (m0, m1), (qaug, ct_ref, row_ref), outs, scratch)
    ml_ref[0:1, :] = scratch[2][...]
    ml_ref[1:2, :] = scratch[3][...]


def stats_far_kernel(m0, m1, qaug, ct_ref, row_ref, ml_ref, near_ref, *rest):
    outs, send_ref, scratch = rest[:7], rest[7], rest[8:]
    scratch[2][...] = ml_ref[0:1, :]
    scratch[3][...] = ml_ref[1:2, :]
    totals_of(HALF, BACK, (m0, m1), (qaug, ct_ref, row_ref), outs, scratch)
    lse = scratch[2][...] + jnp.log2(scratch[3][...])
    totals = outs[5][0:1, :] + near_ref[0:1, :]
    for k in range(NKEYS):
        send_ref[k, 0:1, :] = lse
        send_ref[k, 1:2, 0:128] = totals


def scale_kernel(recv_ref, st_ref, dd_ref, row_ref, ct_ref, mn_ref, mf_ref, dn_ref, df_ref,
                 gs_ref, h_ref, scal_ref, aug_ref, g_ref, eo_ref):
    kk = lax.axis_index(KEYS)
    parts = [recv_ref[k, 0:1, :] for k in range(NKEYS)]
    top = functools.reduce(jnp.maximum, parts)
    lse = top + jnp.log2(sum(jnp.exp2(p - top) for p in parts))
    totals = jnp.concatenate([recv_ref[k, 1:2, 0:128] for k in range(NKEYS)], axis=0)
    dev, lane = iota((NKEYS, 128), 0), iota((NKEYS, 128), 1)
    away = 8 * shift_of(lane, dev) - chunk_of(lane, dev)
    offs = []
    for n in range(BACK):
        nearer = (lane < BACK) & (away < 8 * shift_of(n, kk) - chunk_of(n, kk))
        off = total_of(jnp.where(nearer, totals, 0.0))
        offs.append((n, jnp.broadcast_to(off, (1, 128))))
    eo = jnp.exp2(LOG2E * stacked_rows(offs, 8, 128))
    eo_ref[0:8, :] = jnp.concatenate([eo] * 4, axis=1)
    eo_ref[8:16, :] = jnp.zeros((8, TQ), F32)
    seg = row_ref[1:2, :]
    inside, u = row_factor(row_ref)
    beta = (LOG2E * row_ref[0:1, :] - lse) * (1.0 / CS)
    rows = [(n, 1.0) for n in range(3)]
    rows += [(4 + n, part) for n, part in enumerate(split3(jnp.where(inside, beta, NEG)))]
    rows += [(7 + n, part) for n, part in enumerate(split3(beta))]
    rows += [(10 + n, jnp.where(seg == float(n), 0.0, NEG)) for n in range(4)]
    aug_ref[...] = stacked_rows(rows, 16, QR).astype(BF16)
    ctf = ct_ref[...].astype(F32)
    h = h_ref[...]
    g_all = jnp.zeros((STATE, STATE), F32)
    ast = []
    for n in range(BACK):
        weighted = gs_ref[n % HALF, :, (n // HALF) * 64 : (n // HALF) * 64 + 64] * (eo[n : n + 1, 0:64] * eo[n : n + 1, 0:64])
        g_all = g_all + weighted
        ast.append(total_of(weighted * h) * (2.0 / SEQ))
    g_all = g_all * (2.0 / SEQ)
    g_ref[...] = g_all
    os = dot(left_three(g_all), right_three(ctf * (u * u)))
    near = dd_ref[1:2, :] * (2.0 / SEQ) - 2.0 * jnp.exp2(st_ref[0:1, :] - lse) * dd_ref[0:1, :]
    mref = jnp.concatenate([mn_ref[0:HALF, :], mf_ref[0:HALF, :]], axis=0)
    d = jnp.concatenate([dn_ref[0:HALF, :], df_ref[0:HALF, :]], axis=0)
    far = jnp.where(inside, jnp.exp2(mref - lse) * u * d, 0.0)
    far = -2.0 * eo[:, 0:1] * far
    along = near + jnp.sum(ctf * os, axis=0, keepdims=True) + jnp.sum(far, axis=0, keepdims=True)
    far = jnp.sum(far, axis=1, keepdims=True)
    lane = iota((1, 128), 1)
    out = jnp.where(lane == 0, total_of(near), 0.0)
    for n in range(BACK):
        out = jnp.where(lane == n + 1, far[n : n + 1, :] + ast[n], out)
    for q in range(NKEYS):
        part = jnp.sum(along[:, q * KB : (q + 1) * KB], axis=1, keepdims=True)
        out = jnp.where(lane == 16 + q, part, out)
    scal_ref[...] = jnp.broadcast_to(out, (NROWS * NKEYS, 128))


def gradients(start, stop, refs, outs, o_acc, scratch):
    nb_ref, kaug, bts, h_ref, v_ref, qaug_ref, aug_ref, ct_ref, row_ref, eo_ref = refs
    qaug, g_acc, s_a, s_b, h_a, h_b, l_a, l_b = scratch
    kk = lax.axis_index(KEYS)
    padded(qaug_ref, qaug)
    qaug[128:144, :] = aug_ref[...]
    g_acc[...] = jnp.zeros_like(g_acc)
    count = nb_ref[0]
    empty = stop - start
    tiles = tiles_in(row_ref)

    def scores(pos, s_buf):
        s_buf[...] = dot(kaug[pos[0]], qaug[:, lanes(pos)])

    def weigh(s_buf, h_buf, l_buf):
        hi, lo = split2(jnp.exp2(CS * s_buf[...]))
        h_buf[...] = hi
        l_buf[...] = lo

    def add(pos, h_buf, l_buf):
        sl = lanes(pos)
        c, b = ct_ref[:, sl], bts[pos[0]]
        g = dot_nt(c, h_buf[...]) + dot_nt(c, l_buf[...])
        g_acc[pl.ds(pos[0], 1)] += g.reshape(1, STATE, KB)
        o = dot(b, h_buf[...]) + dot(b, l_buf[...])
        o_acc[:, sl] += o * eo_ref[pl.ds(pos[0] + start, 1), :]

    @pl.when(count > 0)
    def _():
        first = (jnp.int32(0), jnp.int32(0))
        scores(first, s_a)
        weigh(s_a, h_a, l_a)
        second = after(first, count, tiles, empty)
        scores(second, s_b)

        def step(_, carry):
            pos, second = carry[:2], carry[2:]
            third = after(second, count, tiles, empty)
            fourth = after(third, count, tiles, empty)
            add(pos, h_a, l_a)
            weigh(s_b, h_b, l_b)
            scores(third, s_a)
            add(second, h_b, l_b)
            weigh(s_a, h_a, l_a)
            scores(fourth, s_b)
            return (*third, *fourth)

        lax.fori_loop(0, (count * tiles + 1) // 2, step, (*first, *second))

    h_left = left_three(h_ref[...])
    for n in range(start, stop):
        e = eo_ref[n : n + 1, 0:KB]
        v = v_ref[n - start : n - start + 1, :] * e
        student = dot(h_left, right_three(bts[n - start].astype(F32) * v)) * v
        out = pl.ds(pl.multiple_of(slot_of(n, kk) * STATE, STATE), STATE)
        outs[(n - start) // 2][out, :] = (2.0 / SEQ) * student - 2.0 * e * g_acc[n - start]


def far_kernel(*refs):
    o_ref = refs[12]
    o_ref[...] = jnp.zeros_like(o_ref)
    gradients(HALF, BACK, refs[:10], refs[10:12], o_ref, refs[13:])


def near_kernel(*refs):
    g_ref, kd_ref, btd_ref, own_ref, o_ref = refs[10:15]
    gb_ref, gc_ref, o_acc, *scratch = refs[17:]
    o_acc[...] = o_ref[...]
    gradients(0, HALF, refs[:10], refs[15:17], o_acc, scratch)
    qaug, ct_ref, row_ref = scratch[0], refs[7], refs[8]
    kk = lax.axis_index(KEYS)
    gb_ref[...] = jnp.zeros_like(gb_ref)
    bt = btd_ref[...]
    cols = own_columns(own_ref)
    b = jnp.transpose(bt.astype(F32)).astype(BF16)

    def chunk(q, carry):
        sl = pl.ds(pl.multiple_of(q * KB, KB), KB)
        seen, wi, w = weighted(q - kk, b, cols, row_ref, ct_ref, sl)
        p = jnp.where(seen, jnp.exp2(CS * dot(kd_ref[...], qaug[:, sl])), 0.0)
        hi, lo = split2(p - w * wi * (1.0 / SEQ))
        c = ct_ref[:, sl]
        gb_ref[...] -= 2.0 * (dot_nt(c, hi) + dot_nt(c, lo))
        o_acc[:, sl] += dot(bt, hi) + dot(bt, lo)
        return carry

    lax.fori_loop(kk, NKEYS, chunk, 0)
    _, u = row_factor(row_ref)
    os = dot(left_three(g_ref[...]), right_three(ct_ref[...].astype(F32) * (u * u)))
    for k in range(NKEYS):
        sl = slice(k * KB, (k + 1) * KB)
        gc_ref[k] = os[:, sl] - 2.0 * o_acc[:, sl]


def final_kernel(*refs):
    got = refs[: HALF // 2]
    swap_ref, gb_ref, gc_ref, scal_ref, bt_ref, ct_ref, out_c, out_b, out_d = refs[HALF // 2 :]
    row, kk = lax.axis_index(ROWS), lax.axis_index(KEYS)
    gb = functools.reduce(jnp.add, [g[0:STATE, :] for g in got]) + gb_ref[...] + swap_ref[...]
    gc = functools.reduce(jnp.add, [gc_ref[k] for k in range(NKEYS)])
    out_b[...] = gb
    out_c[...] = gc
    c = ct_ref[:, pl.ds(pl.multiple_of(kk * KB, KB), KB)].astype(F32)
    lead = jnp.sum(c * gc - bt_ref[...].astype(F32) * gb, axis=0, keepdims=True)
    later = (iota((KB, KB), 0) >= iota((KB, KB), 1)).astype(F32)
    local = dotx(jnp.broadcast_to(lead, (8, KB)), later)
    me = row * NKEYS + kk
    dev, lane = iota((128, 128), 0), iota((128, 128), 1)
    at, block = dev % NKEYS, lane - 1
    first = dev - at
    chunk = first - NKEYS * shift_of(block, at) + chunk_of(block, at)
    chunk = jnp.where(lane >= 16, first + lane - 16, jnp.where(lane == 0, dev, chunk))
    sign = jnp.where(lane <= BACK, -1.0, jnp.where((lane >= 16) & (lane < 24), 1.0, 0.0))
    tail = total_of(jnp.where(chunk > me, sign * scal_ref[...], 0.0))
    out_d[...] = (local[0:1, :] + tail) * (1.0 / SEQ)


def call(kernel, **how):
    params = pltpu.CompilerParams(vmem_limit_bytes=20 * 1024 * 1024)
    return pl.pallas_call(kernel, compiler_params=params, **how)


def sds(shape, dtype=F32):
    return jax.ShapeDtypeStruct(shape, dtype)


def vmem():
    return pl.BlockSpec(memory_space=pltpu.VMEM)


def smem():
    return pl.BlockSpec(memory_space=pltpu.SMEM)


PAIRS = [(k, k ^ 1) for k in range(NKEYS)]
HOP_PAIRS = [
    [
        (r * NKEYS + k, (r + shift_of(2 * j, k)) * NKEYS + k)
        for r in range(NROWS)
        for k in range(NKEYS)
        if r + shift_of(2 * j, k) < NROWS
    ]
    for j in range(HALF // 2)
]
ONWARD = [(r, r + HALF) for r in range(NROWS - HALF)]


def on_device(queries, keys_in, c_proj, b_proj, log_decay, segments):
    ct, bt = c_proj.T, b_proj.T
    x, msg, pair = pl.pallas_call(
        send_kernel, out_shape=(sds((NKEYS, 4, 128)), sds((MSG, 128), BF16), sds((2 * MSG, 128), BF16)),
        name="send",
    )(log_decay.reshape(2, 128), segments.reshape(2, 128), keys_in, bt)
    x = lax.all_to_all(x, KEYS, 0, 0, tiled=True)
    other = lax.ppermute(msg, KEYS, PAIRS)
    pair = lax.dynamic_update_slice(pair, other, (MSG, 0))
    msgs = [lax.ppermute(pair, BOTH, hop) for hop in HOP_PAIRS]
    onward = [lax.ppermute(msg, ROWS, ONWARD) for msg in msgs]
    rowmeta, qaug, kd, own, st = call(
        diag_kernel,
        out_shape=(
            sds((8, QR)), sds((144, QR), BF16), sds((KB, 256), BF16), sds((8, KB)),
            sds((8, QR)),
        ),
        scratch_shapes=[pltpu.VMEM((256, QR), BF16)],
        name="diag",
    )(x, msg, queries)

    def stats(kernel, last, name):
        return call(
            kernel,
            out_shape=(
                sds((8, QR)), sds((8, QR)), sds((HALF + 1, KB, 256), BF16),
                sds((HALF + 1, STATE, KB), BF16), sds((1,), jnp.int32), sds((8, 128)),
                sds((8, KB)), last,
            ),
            out_specs=(*[vmem()] * 4, smem(), *[vmem()] * 3),
            scratch_shapes=[
                pltpu.VMEM((HALF + 1, KB, 128), BF16), pltpu.VMEM((128, QR), BF16),
                pltpu.VMEM((1, QR), F32), pltpu.VMEM((1, QR), F32),
                *[pltpu.VMEM((KB, TQ), F32)] * 4, pltpu.VMEM((256, QR), BF16),
            ],
            name=name,
        )

    mn, dn, *parts_near, sums, vn, ml = stats(stats_near_kernel, sds((8, QR)), "statsnear")(
        *msgs, qaug, ct, rowmeta, st
    )
    mf, df, *parts_far, _, vf, send = stats(stats_far_kernel, sds((NKEYS, 2, QR)), "statsfar")(
        *onward, qaug, ct, rowmeta, ml, sums
    )
    recv = lax.all_to_all(send, KEYS, 0, 0, tiled=True)
    h, dd, gs = call(
        student_kernel,
        out_shape=(
            sds((STATE, STATE)), sds((8, QR)),
            sds((HALF, STATE, 2 * STATE)),
        ),
        scratch_shapes=[pltpu.VMEM((256, QR), BF16)],
        name="student",
    )(parts_near[1], parts_far[1], vn, vf, qaug, kd, own, st, rowmeta, ct, bt)
    scal, aug, g, eo = call(
        scale_kernel,
        out_shape=(
            sds((NROWS * NKEYS, 128)), sds((16, QR), BF16), sds((STATE, STATE)),
            sds((16, TQ)),
        ),
        name="scale",
    )(recv, st, dd, rowmeta, ct, mn, mf, dn, df, gs, h)
    scal = lax.all_to_all(scal, BOTH, 0, 0, tiled=True)

    def shared(parts, v):
        kaug, bts, nb = parts
        return nb, kaug, bts, h, v, qaug, aug, ct, rowmeta, eo

    scratch = [
        pltpu.VMEM((256, QR), BF16), pltpu.VMEM((HALF + 1, STATE, KB), F32),
        *[pltpu.VMEM((KB, TQ), F32)] * 2, *[pltpu.VMEM((KB, TQ), BF16)] * 4,
    ]
    *far, o = call(
        far_kernel,
        in_specs=[smem(), *[vmem()] * 9],
        out_shape=(*[sds((2 * STATE, KB))] * 2, sds((STATE, QR))),
        scratch_shapes=scratch,
        name="far",
    )(*shared(parts_far, vf))
    far = [lax.ppermute(g, ROWS, [(b, a) for a, b in ONWARD]) for g in far]
    *near, gb, gc = call(
        near_kernel,
        in_specs=[smem(), *[vmem()] * 14],
        out_shape=(*[sds((2 * STATE, KB))] * 2, sds((STATE, KB)), sds((NKEYS, STATE, KB))),
        scratch_shapes=[pltpu.VMEM((STATE, QR), F32), *scratch],
        name="near",
    )(*shared(parts_near, vn), g, kd, bt, own, o)
    gc = lax.all_to_all(gc, KEYS, 0, 0, tiled=True)
    back = [
        lax.ppermute(g + h, BOTH, [(b, a) for a, b in hop])
        for g, h, hop in zip(near, far, HOP_PAIRS)
    ]
    other = functools.reduce(jnp.add, [g[STATE:, :] for g in back])
    other = lax.ppermute(other, KEYS, PAIRS)
    out_c, out_b, out_d = call(
        final_kernel,
        out_shape=(sds((STATE, KB)), sds((STATE, KB)), sds((1, KB))),
        name="final",
    )(*back, other, gb, gc, scal, bt, ct)
    return out_c.T, out_b.T, out_d.reshape(KB)


def solution(mesh):
    return jax.shard_map(
        on_device,
        mesh=mesh,
        in_specs=(
            P(ROWS, None), P(BOTH, None), P(ROWS, None), P(BOTH, None), P(BOTH), P(BOTH),
        ),
        out_specs=(P(BOTH, None), P(BOTH, None), P(BOTH)),
        check_vma=False,
    )
```

```python
import functools

import jax
import jax.numpy as jnp
from jax import lax
from jax.experimental import pallas as pl
from jax.experimental.pallas import tpu as pltpu
from jax.sharding import PartitionSpec as P


ROWS = "rows"
KEYS = "keys"
BOTH = ("rows", "keys")
BACK = 8
HALF = BACK // 2
NROWS = 16
NKEYS = 8
KB = 256
QR = KB * NKEYS
HEAD = 128
STATE = 64
SEQ = QR * NROWS
LOG2E = 1.4426950408889634
CS = HEAD**-0.5 * LOG2E
NEG = -1e30
TQ = 512
MSG = KB + 128 + 32
F32 = jnp.float32
BF16 = jnp.bfloat16
HI = lax.Precision.HIGHEST


def dot(a, b):
    return jnp.dot(a, b, preferred_element_type=F32)


def dotx(a, b):
    return jnp.dot(a, b, precision=HI, preferred_element_type=F32)


def iota(shape, dim):
    return lax.broadcasted_iota(jnp.int32, shape, dim)


def split2(x):
    hi = x.astype(BF16)
    lo = (x - hi.astype(F32)).astype(BF16)
    return hi, lo


def split3(x):
    hi = x.astype(BF16).astype(F32)
    mid = (x - hi).astype(BF16).astype(F32)
    return hi, mid, x - hi - mid


def total_of(x):
    return jnp.sum(jnp.sum(x, axis=0, keepdims=True), axis=1, keepdims=True)


def dot_nt(a, b):
    return lax.dot_general(a, b, (((1,), (1,)), ((), ())), preferred_element_type=F32)


def stacked_rows(rows, height, width):
    line = iota((height, width), 0)
    out = jnp.zeros((height, width), F32)
    for n, row in rows:
        out = jnp.where(line == n, row, out)
    return out


def columns_of(rows):
    wide = jnp.concatenate([rows, jnp.zeros((112, KB), F32)], axis=0)
    return jnp.transpose(wide)[:, 0:16]


def left_three(x):
    hi, lo = split2(x)
    return jnp.concatenate([hi, hi, lo], axis=1)


def right_three(x):
    hi, lo = split2(x)
    return jnp.concatenate([hi, lo, hi], axis=0)


def row_factor(row_ref):
    seg = row_ref[1:2, :]
    inside = seg == seg[:, 0:1]
    return inside, jnp.where(inside, jnp.exp2(LOG2E * row_ref[0:1, :]), 0.0)


def local_prefix(ld):
    upper = (iota((128, 128), 0) <= iota((128, 128), 1)).astype(F32)
    inside = dotx(jnp.concatenate([ld, jnp.zeros((6, 128), F32)], axis=0), upper)
    first = jnp.broadcast_to(inside[0:1, 127:128], (1, 128))
    second = jnp.broadcast_to(inside[1:2, 127:128], (1, 128))
    return (inside[0:1], inside[1:2] + first), first + second


def padded(src, dst):
    dst[0:144, :] = src[...]
    dst[144:256, :] = jnp.zeros((112, QR), BF16)


def own_columns(own_ref):
    cols = columns_of(jnp.concatenate([own_ref[...], jnp.zeros((8, KB), F32)], axis=0))
    return cols[:, 0:1], cols[:, 1:2]


def send_kernel(ld_ref, seg_ref, k_ref, bt_ref, out_ref, msg_ref, pair_ref):
    label = seg_ref[...].astype(F32)
    for k in range(NKEYS):
        out_ref[k, 0:2, :] = ld_ref[...]
        out_ref[k, 2:4, :] = label
    pre, total = local_prefix(ld_ref[...])
    msg_ref[0:KB, :] = k_ref[...]
    for h in range(2):
        rows = (*split3(total - pre[h]), label[h : h + 1], *split3(total), jnp.ones((1, 128), F32))
        msg_ref[KB + 64 * h : KB + 64 * (h + 1), :] = bt_ref[:, h * 128 : (h + 1) * 128]
        msg_ref[KB + 128 + 16 * h : KB + 144 + 16 * h, :] = stacked_rows(
            enumerate(rows), 16, 128
        ).astype(BF16)
    pair_ref[0:MSG, :] = msg_ref[...]
    pair_ref[MSG:, :] = jnp.zeros((MSG, 128), BF16)


def diag_kernel(x_ref, msg_ref, q_ref, row_ref, qaug_ref, kaug_ref, own_ref, st_ref, qaug):
    kk = lax.axis_index(KEYS)
    ld = jnp.concatenate([x_ref[a, 0:2, :] for a in range(NKEYS)], axis=0)
    sg = jnp.concatenate([x_ref[a, 2:4, :] for a in range(NKEYS)], axis=0)
    upper = (iota((128, 128), 0) <= iota((128, 128), 1)).astype(F32)
    within = dotx(ld, upper)
    tot = jnp.broadcast_to(within[:, 127:128], (16, 128))
    lower = (iota((16, 16), 1) < iota((16, 16), 0)).astype(F32)
    pre = within + dotx(lower, tot)
    row_ref[...] = jnp.zeros_like(row_ref)
    row_ref[0:1, :] = jnp.concatenate([pre[a : a + 1] for a in range(16)], axis=1)
    row_ref[1:2, :] = jnp.concatenate([sg[a : a + 1] for a in range(16)], axis=1)

    def own(arr):
        line = iota((16, 128), 0)
        halves = [
            jnp.sum(jnp.where(line == 2 * kk + h, arr, 0.0), axis=0, keepdims=True)
            for h in range(2)
        ]
        return jnp.concatenate(halves, axis=1)

    own_pre, own_seg = own(pre), own(sg)
    seg = row_ref[1:2, :]
    inside, _ = row_factor(row_ref)
    qaug_ref[0:128, :] = jnp.transpose(q_ref[...])
    doc_rows = [(10 + n, jnp.where(seg == float(n), 0.0, NEG)) for n in range(4)]
    qaug_ref[128:144, :] = stacked_rows(
        [(3, 1.0), (4, jnp.where(inside, 0.0, NEG)), *doc_rows], 16, QR
    ).astype(BF16)
    padded(qaug_ref, qaug)
    rows = list(enumerate(split3(own_pre * (-LOG2E / CS))))
    rows += [(7 + n, 1.0) for n in range(3)]
    rows += [(10 + n, jnp.where(own_seg == float(n), 1.0, 0.0)) for n in range(4)]
    cols = columns_of(stacked_rows(rows, 16, KB))
    kaug_ref[:, 0:128] = msg_ref[0:KB, :]
    kaug_ref[:, 128:256] = jnp.zeros((KB, 128), BF16)
    kaug_ref[:, 128:144] = cols.astype(BF16)
    own_ref[...] = stacked_rows([(0, own_pre), (1, own_seg)], 8, KB)
    st_ref[0:1, :] = jnp.full((1, QR), NEG, F32)
    st_ref[1:2, :] = jnp.ones((1, QR), F32)
    st_ref[2:8, :] = jnp.zeros((6, QR), F32)

    def chunk(q, carry):
        sl = pl.ds(pl.multiple_of(q * TQ, TQ), TQ)
        causal = iota((KB, TQ), 0) <= iota((KB, TQ), 1) + (q * TQ - kk * KB)
        s = jnp.where(causal, dot(kaug_ref[...], qaug[:, sl]), NEG)
        top = jnp.max(s, axis=0, keepdims=True) * CS
        st_ref[0:1, sl] = top
        st_ref[1:2, sl] = jnp.sum(jnp.exp2(s * CS - top), axis=0, keepdims=True)
        return carry

    lax.fori_loop(kk * KB // TQ, QR // TQ, chunk, 0)


def slot_of(n, kk):
    return (n + 1 + kk) % 2


def shift_of(n, kk):
    return 2 * (n // 2) + 1 + kk % 2


def chunk_of(n, kk):
    return kk - kk % 2 + 1 - n % 2


def message(msgs, start, i, kk, doc):
    base = pl.multiple_of(slot_of(start + i, kk) * MSG, MSG)
    msg = msgs[i // 2].at[pl.ds(base, MSG)]
    meta = jnp.concatenate(
        [msg[KB + 128 : KB + 144, :], msg[KB + 144 : KB + 160, :]], axis=1
    ).astype(F32)
    bt = jnp.concatenate([msg[KB : KB + 64, :], msg[KB + 64 : KB + 128, :]], axis=1)
    seen = (meta[3:4] == doc) & (meta[7:8] > 0.0)
    here = LOG2E * (meta[0:1] + meta[1:2] + meta[2:3])
    total = meta[4:5, 0:128] + meta[5:6, 0:128] + meta[6:7, 0:128]
    return msg, bt, seen, here, jnp.where(seen, jnp.exp2(here), 0.0), total


def weighted(ahead, b, cols, row_ref, ct_ref, sl):
    shape = (KB, sl.size)
    causal = iota(shape, 0) <= iota(shape, 1) + ahead
    seen = causal & (cols[1] == row_ref[1:2, sl])
    w = jnp.exp2(LOG2E * (row_ref[0:1, sl] - cols[0]))
    w = jnp.where(seen, w, 0.0)
    return seen, w * dot(b, ct_ref[:, sl]), w


def student_kernel(*refs):
    (btn_ref, btf_ref, vn_ref, vf_ref, qaug_ref, kaug_ref, own_ref, st_ref, row_ref, ct_ref, bt_ref,
     h_ref, dd_ref, gs_ref, qaug) = refs
    padded(qaug_ref, qaug)
    kk = lax.axis_index(KEYS)
    _, u = row_factor(row_ref)
    hi, lo = split2(ct_ref[...].astype(F32) * (u * u))
    h = dot_nt(hi, ct_ref[...]) + dot_nt(lo, ct_ref[...])
    h_ref[...] = h
    for n in range(BACK):
        bts, vs = (btn_ref, vn_ref) if n < HALF else (btf_ref, vf_ref)
        v = vs[n % HALF : n % HALF + 1, :]
        bv = bts[n % HALF].astype(F32) * v
        hi, lo = split2(bv)
        both = jnp.concatenate([hi, lo], axis=0)
        g = dot_nt(both, both)
        g = g[0:64, 0:64] + g[0:64, 64:128] + g[64:128, 0:64] + g[64:128, 64:128]
        gs_ref[n % HALF, :, (n // HALF) * 64 : (n // HALF) * 64 + 64] = g
    dd_ref[...] = jnp.zeros_like(dd_ref)
    cols = own_columns(own_ref)
    b = jnp.transpose(bt_ref[...].astype(F32)).astype(BF16)

    def chunk(q, carry):
        sl = pl.ds(pl.multiple_of(q * TQ, TQ), TQ)
        seen, wi, _ = weighted(q * TQ - kk * KB, b, cols, row_ref, ct_ref, sl)
        e = jnp.exp2(dot(kaug_ref[...], qaug[:, sl]) * CS - st_ref[0:1, sl])
        dd_ref[0:1, sl] = jnp.sum(jnp.where(seen, e, 0.0) * wi, axis=0, keepdims=True)
        dd_ref[1:2, sl] = jnp.sum(wi * wi, axis=0, keepdims=True)
        return carry

    lax.fori_loop(kk * KB // TQ, QR // TQ, chunk, 0)


def tiles_in(row_ref):
    seg = row_ref[1:2, :]
    count = jnp.sum(jnp.where(seg == seg[:, 0:1], 1.0, 0.0))
    return (count.astype(jnp.int32) + (TQ - 1)) // TQ


def after(pos, many, tiles, empty):
    n, t = pos
    wrap = t + 1 >= tiles
    n = jnp.where(wrap, n + 1, n)
    return jnp.where(n >= many, empty, n), jnp.where(wrap, 0, t + 1)


def lanes(pos):
    return pl.ds(pl.multiple_of(pos[1] * TQ, TQ), TQ)


def totals_of(start, stop, msgs, refs, outs, scratch):
    qaug, ct_ref, row_ref = refs
    mref_ref, d_ref, kaug, bts_ref, nb_ref, sum_ref, v_ref = outs
    bl, cc, m_acc, l_acc, s_a, s_b, i_a, i_b, qpad = scratch
    padded(qaug, qpad)
    kk = lax.axis_index(KEYS)
    doc = row_ref[1:2, 0:1]
    mref_ref[...] = jnp.full_like(mref_ref, NEG)
    d_ref[...] = jnp.zeros_like(d_ref)
    cc[0:64, :] = ct_ref[...]
    cc[64:128, :] = ct_ref[...]
    lane = iota((KB, 128), 1)
    empty = stop - start
    kaug[empty, :, 0:128] = jnp.zeros((KB, 128), BF16)
    kaug[empty, :, 128:256] = jnp.where((lane == 0) | (lane == 3), NEG, 0.0).astype(BF16)
    bts_ref[empty] = jnp.zeros((STATE, KB), BF16)
    bl[empty] = jnp.zeros((KB, 128), BF16)
    count = jnp.int32(0)
    lane1 = iota((1, 128), 1)
    totals = jnp.zeros((1, 128), F32)
    for i in range(stop - start):
        msg, bt, seen, here, v, total = message(msgs, start, i, kk, doc)
        totals = jnp.where(lane1 == start + i, total, totals)
        active = jnp.max(jnp.where(seen, 1.0, 0.0)) > 0.0
        count = count + active.astype(jnp.int32)
        rows = list(enumerate(split3(jnp.where(seen, here * (1.0 / CS), NEG))))
        rows += [(3, jnp.where(seen, 0.0, NEG)), (4, 1.0), (5, 1.0), (6, 1.0)]
        kaug[i, :, 0:128] = msg[0:KB, :]
        kaug[i, :, 128:256] = jnp.zeros((KB, 128), BF16)
        kaug[i, :, 128:144] = columns_of(stacked_rows(rows, 16, KB)).astype(BF16)
        bts_ref[i] = bt
        v_ref[i : i + 1, :] = v
        bv = bt.astype(F32) * v
        hi = bv.astype(BF16).astype(F32)
        bl[i] = jnp.transpose(jnp.concatenate([hi, bv - hi], axis=0)).astype(BF16)

    nb_ref[0] = count
    sum_ref[...] = jnp.broadcast_to(totals, (8, 128))
    tiles = tiles_in(row_ref)

    def scores(pos, s_buf, i_buf):
        s_buf[...] = dot(kaug[pos[0]], qpad[:, lanes(pos)])
        i_buf[...] = dot(bl[pos[0]], cc[:, lanes(pos)])

    def work(pos, s_buf, i_buf):
        sl = lanes(pos)
        old = m_acc[:, sl]
        new = jnp.maximum(old, jnp.max(s_buf[...], axis=0, keepdims=True) * CS)
        e = jnp.exp2(s_buf[...] * CS - new)
        l_acc[:, sl] = l_acc[:, sl] * jnp.exp2(old - new) + jnp.sum(e, axis=0, keepdims=True)
        m_acc[:, sl] = new
        mref_ref[pl.ds(pos[0], 1), sl] = new
        d_ref[pl.ds(pos[0], 1), sl] = jnp.sum(e * i_buf[...], axis=0, keepdims=True)

    @pl.when(count > 0)
    def _():
        first = (jnp.int32(0), jnp.int32(0))
        scores(first, s_a, i_a)

        def step(_, pos):
            second = after(pos, count, tiles, empty)
            third = after(second, count, tiles, empty)
            scores(second, s_b, i_b)
            work(pos, s_a, i_a)
            scores(third, s_a, i_a)
            work(second, s_b, i_b)
            return third

        lax.fori_loop(0, (count * tiles + 1) // 2, step, first)


def stats_near_kernel(m0, m1, qaug, ct_ref, row_ref, st_ref, *rest):
    outs, ml_ref, scratch = rest[:7], rest[7], rest[8:]
    scratch[2][...] = st_ref[0:1, :]
    scratch[3][...] = st_ref[1:2, :]
    totals_of(0, HALF, (m0, m1), (qaug, ct_ref, row_ref), outs, scratch)
    ml_ref[0:1, :] = scratch[2][...]
    ml_ref[1:2, :] = scratch[3][...]


def stats_far_kernel(m0, m1, qaug, ct_ref, row_ref, ml_ref, near_ref, *rest):
    outs, send_ref, scratch = rest[:7], rest[7], rest[8:]
    scratch[2][...] = ml_ref[0:1, :]
    scratch[3][...] = ml_ref[1:2, :]
    totals_of(HALF, BACK, (m0, m1), (qaug, ct_ref, row_ref), outs, scratch)
    lse = scratch[2][...] + jnp.log2(scratch[3][...])
    totals = outs[5][0:1, :] + near_ref[0:1, :]
    for k in range(NKEYS):
        send_ref[k, 0:1, :] = lse
        send_ref[k, 1:2, 0:128] = totals


def scale_kernel(recv_ref, st_ref, dd_ref, row_ref, ct_ref, mn_ref, mf_ref, dn_ref, df_ref,
                 gs_ref, h_ref, scal_ref, aug_ref, g_ref, eo_ref):
    kk = lax.axis_index(KEYS)
    parts = [recv_ref[k, 0:1, :] for k in range(NKEYS)]
    top = functools.reduce(jnp.maximum, parts)
    lse = top + jnp.log2(sum(jnp.exp2(p - top) for p in parts))
    totals = jnp.concatenate([recv_ref[k, 1:2, 0:128] for k in range(NKEYS)], axis=0)
    dev, lane = iota((NKEYS, 128), 0), iota((NKEYS, 128), 1)
    away = 8 * shift_of(lane, dev) - chunk_of(lane, dev)
    offs = []
    for n in range(BACK):
        nearer = (lane < BACK) & (away < 8 * shift_of(n, kk) - chunk_of(n, kk))
        off = total_of(jnp.where(nearer, totals, 0.0))
        offs.append((n, jnp.broadcast_to(off, (1, 128))))
    eo = jnp.exp2(LOG2E * stacked_rows(offs, 8, 128))
    eo_ref[0:8, :] = jnp.concatenate([eo] * 4, axis=1)
    eo_ref[8:16, :] = jnp.zeros((8, TQ), F32)
    seg = row_ref[1:2, :]
    inside, u = row_factor(row_ref)
    beta = (LOG2E * row_ref[0:1, :] - lse) * (1.0 / CS)
    rows = [(n, 1.0) for n in range(3)]
    rows += [(4 + n, part) for n, part in enumerate(split3(jnp.where(inside, beta, NEG)))]
    rows += [(7 + n, part) for n, part in enumerate(split3(beta))]
    rows += [(10 + n, jnp.where(seg == float(n), 0.0, NEG)) for n in range(4)]
    aug_ref[...] = stacked_rows(rows, 16, QR).astype(BF16)
    ctf = ct_ref[...].astype(F32)
    h = h_ref[...]
    g_all = jnp.zeros((STATE, STATE), F32)
    ast = []
    for n in range(BACK):
        weighted = gs_ref[n % HALF, :, (n // HALF) * 64 : (n // HALF) * 64 + 64] * (eo[n : n + 1, 0:64] * eo[n : n + 1, 0:64])
        g_all = g_all + weighted
        ast.append(total_of(weighted * h) * (2.0 / SEQ))
    g_all = g_all * (2.0 / SEQ)
    g_ref[...] = g_all
    os = dot(left_three(g_all), right_three(ctf * (u * u)))
    near = dd_ref[1:2, :] * (2.0 / SEQ) - 2.0 * jnp.exp2(st_ref[0:1, :] - lse) * dd_ref[0:1, :]
    mref = jnp.concatenate([mn_ref[0:HALF, :], mf_ref[0:HALF, :]], axis=0)
    d = jnp.concatenate([dn_ref[0:HALF, :], df_ref[0:HALF, :]], axis=0)
    far = jnp.where(inside, jnp.exp2(mref - lse) * u * d, 0.0)
    far = -2.0 * eo[:, 0:1] * far
    along = near + jnp.sum(ctf * os, axis=0, keepdims=True) + jnp.sum(far, axis=0, keepdims=True)
    far = jnp.sum(far, axis=1, keepdims=True)
    lane = iota((1, 128), 1)
    out = jnp.where(lane == 0, total_of(near), 0.0)
    for n in range(BACK):
        out = jnp.where(lane == n + 1, far[n : n + 1, :] + ast[n], out)
    for q in range(NKEYS):
        part = jnp.sum(along[:, q * KB : (q + 1) * KB], axis=1, keepdims=True)
        out = jnp.where(lane == 16 + q, part, out)
    scal_ref[...] = jnp.broadcast_to(out.reshape(1, 1, 128), (NKEYS, 8, 128))


def row_sums(scal_ref):
    return jnp.concatenate([scal_ref[k, 0:1, :] for k in range(NKEYS)], axis=0)


def crossing(sums, away):
    dev, lane = iota((NKEYS, 128), 0), iota((NKEYS, 128), 1)
    block = lane - 1
    blocks = (lane >= 1) & (lane <= BACK)
    past = blocks & (shift_of(block, dev) >= away)
    here = blocks & (shift_of(block, dev) == away)
    place = iota((1, KB), 1)
    row = jnp.where(place == 0, total_of(jnp.where(past, sums, 0.0)), 0.0)
    for q in range(NKEYS):
        part = total_of(jnp.where(here & (chunk_of(block, dev) == q), sums, 0.0))
        row = jnp.where(place == 8 + q, part, row)
    return jnp.broadcast_to(row, (8, KB))


def gradients(start, stop, refs, scal_ref, outs, o_acc, scratch):
    nb_ref, kaug, bts, h_ref, v_ref, qaug_ref, aug_ref, ct_ref, row_ref, eo_ref = refs
    qaug, g_acc, s_a, s_b, h_a, h_b, l_a, l_b = scratch
    kk = lax.axis_index(KEYS)
    padded(qaug_ref, qaug)
    qaug[128:144, :] = aug_ref[...]
    g_acc[...] = jnp.zeros_like(g_acc)
    count = nb_ref[0]
    empty = stop - start
    tiles = tiles_in(row_ref)

    def scores(pos, s_buf):
        s_buf[...] = dot(kaug[pos[0]], qaug[:, lanes(pos)])

    def weigh(s_buf, h_buf, l_buf):
        hi, lo = split2(jnp.exp2(CS * s_buf[...]))
        h_buf[...] = hi
        l_buf[...] = lo

    def add(pos, h_buf, l_buf):
        sl = lanes(pos)
        c, b = ct_ref[:, sl], bts[pos[0]]
        g = dot_nt(c, h_buf[...]) + dot_nt(c, l_buf[...])
        g_acc[pl.ds(pos[0], 1)] += g.reshape(1, STATE, KB)
        o = dot(b, h_buf[...]) + dot(b, l_buf[...])
        o_acc[:, sl] += o * eo_ref[pl.ds(pos[0] + start, 1), :]

    @pl.when(count > 0)
    def _():
        first = (jnp.int32(0), jnp.int32(0))
        scores(first, s_a)
        weigh(s_a, h_a, l_a)
        second = after(first, count, tiles, empty)
        scores(second, s_b)

        def step(_, carry):
            pos, second = carry[:2], carry[2:]
            third = after(second, count, tiles, empty)
            fourth = after(third, count, tiles, empty)
            scores(third, s_a)
            weigh(s_b, h_b, l_b)
            add(pos, h_a, l_a)
            scores(fourth, s_b)
            weigh(s_a, h_a, l_a)
            add(second, h_b, l_b)
            return (*third, *fourth)

        lax.fori_loop(0, (count * tiles + 1) // 2, step, (*first, *second))

    h_left = left_three(h_ref[...])
    for n in range(start, stop):
        e = eo_ref[n : n + 1, 0:KB]
        v = v_ref[n - start : n - start + 1, :] * e
        student = dot(h_left, right_three(bts[n - start].astype(F32) * v)) * v
        out = pl.ds(pl.multiple_of(slot_of(n, kk) * STATE, STATE), STATE)
        if n % 2 == 0:
            outs[(n - start) // 2][2 * STATE :, :] = crossing(row_sums(scal_ref), shift_of(n, kk))
        outs[(n - start) // 2][out, :] = (2.0 / SEQ) * student - 2.0 * e * g_acc[n - start]


def own_kernel(qaug_ref, aug_ref, kd_ref, bt_ref, own_ref, ct_ref, row_ref, o_ref, gb_ref, qaug):
    kk = lax.axis_index(KEYS)
    padded(qaug_ref, qaug)
    qaug[128:144, :] = aug_ref[...]
    o_ref[...] = jnp.zeros_like(o_ref)
    gb_ref[...] = jnp.zeros_like(gb_ref)
    bt = bt_ref[...]
    cols = own_columns(own_ref)
    b = jnp.transpose(bt.astype(F32)).astype(BF16)

    def chunk(q, carry):
        sl = pl.ds(pl.multiple_of(q * KB, KB), KB)
        seen, wi, w = weighted((q - kk) * KB, b, cols, row_ref, ct_ref, sl)
        p = jnp.where(seen, jnp.exp2(CS * dot(kd_ref[...], qaug[:, sl])), 0.0)
        hi, lo = split2(p - w * wi * (1.0 / SEQ))
        c = ct_ref[:, sl]
        gb_ref[...] -= 2.0 * (dot_nt(c, hi) + dot_nt(c, lo))
        o_ref[:, sl] = dot(bt, hi) + dot(bt, lo)
        return carry

    lax.fori_loop(kk, NKEYS, chunk, 0)


def far_kernel(*refs):
    scal_ref, o_in, out0, out1, o_ref, *scratch = refs[10:]
    o_ref[...] = o_in[...]
    gradients(HALF, BACK, refs[:10], scal_ref, (out0, out1), o_ref, scratch)


def near_kernel(*refs):
    scal_ref, o_in, g_ref, out0, out1, gc_ref, o_acc, *scratch = refs[10:]
    ct_ref, row_ref = refs[7], refs[8]
    o_acc[...] = o_in[...]
    gradients(0, HALF, refs[:10], scal_ref, (out0, out1), o_acc, scratch)
    _, u = row_factor(row_ref)
    os = dot(left_three(g_ref[...]), right_three(ct_ref[...].astype(F32) * (u * u)))
    for k in range(NKEYS):
        sl = slice(k * KB, (k + 1) * KB)
        gc_ref[k] = os[:, sl] - 2.0 * o_acc[:, sl]


def final_kernel(*refs):
    got = refs[: HALF // 2]
    swap_ref, gb_ref, gc_ref, scal_ref, bt_ref, ct_ref, out_c, out_b, out_d = refs[HALF // 2 :]
    kk = lax.axis_index(KEYS)
    gb = functools.reduce(jnp.add, [g[0:STATE, :] for g in got]) + gb_ref[...]
    gb = gb + swap_ref[0:STATE, :]
    extra = functools.reduce(jnp.add, [g[2 * STATE : 2 * STATE + 1, :] for g in got])
    extra = extra + swap_ref[STATE : STATE + 1, :]
    gc = functools.reduce(jnp.add, [gc_ref[k] for k in range(NKEYS)])
    out_b[...] = gb
    out_c[...] = gc
    c = ct_ref[:, pl.ds(pl.multiple_of(kk * KB, KB), KB)].astype(F32)
    lead = jnp.sum(c * gc - bt_ref[...].astype(F32) * gb, axis=0, keepdims=True)
    later = (iota((KB, KB), 0) >= iota((KB, KB), 1)).astype(F32)
    local = dotx(jnp.broadcast_to(lead, (8, KB)), later)
    dev, lane, place = iota((NKEYS, 128), 0), iota((NKEYS, 128), 1), iota((1, KB), 1)
    rowwise = (lane > 16 + kk) & (lane < 16 + NKEYS)
    sign = jnp.where(rowwise, 1.0, jnp.where((lane == 0) & (dev > kk), -1.0, 0.0))
    passed = jnp.where((place > 8 + kk) & (place < 8 + NKEYS), -1.0, jnp.where(place == 0, 1.0, 0.0))
    tail = total_of(sign * row_sums(scal_ref)) + total_of(passed * extra)
    out_d[...] = (local[0:1, :] + tail) * (1.0 / SEQ)


def call(kernel, **how):
    params = pltpu.CompilerParams(vmem_limit_bytes=20 * 1024 * 1024)
    return pl.pallas_call(kernel, compiler_params=params, **how)


def sds(shape, dtype=F32):
    return jax.ShapeDtypeStruct(shape, dtype)


def vmem():
    return pl.BlockSpec(memory_space=pltpu.VMEM)


def smem():
    return pl.BlockSpec(memory_space=pltpu.SMEM)


PAIRS = [(k, k ^ 1) for k in range(NKEYS)]
HOP_PAIRS = [
    [
        (r * NKEYS + k, (r + shift_of(2 * j, k)) * NKEYS + k)
        for r in range(NROWS)
        for k in range(NKEYS)
        if r + shift_of(2 * j, k) < NROWS
    ]
    for j in range(HALF // 2)
]
ONWARD = [(r, r + HALF) for r in range(NROWS - HALF)]


def on_device(queries, keys_in, c_proj, b_proj, log_decay, segments):
    ct, bt = c_proj.T, b_proj.T
    x, msg, pair = pl.pallas_call(
        send_kernel, out_shape=(sds((NKEYS, 4, 128)), sds((MSG, 128), BF16), sds((2 * MSG, 128), BF16)),
        name="send",
    )(log_decay.reshape(2, 128), segments.reshape(2, 128), keys_in, bt)
    x = lax.all_to_all(x, KEYS, 0, 0, tiled=True)
    other = lax.ppermute(msg, KEYS, PAIRS)
    pair = lax.dynamic_update_slice(pair, other, (MSG, 0))
    msgs = [lax.ppermute(pair, BOTH, hop) for hop in HOP_PAIRS]
    onward = [lax.ppermute(msg, ROWS, ONWARD) for msg in msgs]
    rowmeta, qaug, kd, own, st = call(
        diag_kernel,
        out_shape=(
            sds((8, QR)), sds((144, QR), BF16), sds((KB, 256), BF16), sds((8, KB)),
            sds((8, QR)),
        ),
        scratch_shapes=[pltpu.VMEM((256, QR), BF16)],
        name="diag",
    )(x, msg, queries)

    def stats(kernel, last, name):
        return call(
            kernel,
            out_shape=(
                sds((8, QR)), sds((8, QR)), sds((HALF + 1, KB, 256), BF16),
                sds((HALF + 1, STATE, KB), BF16), sds((1,), jnp.int32), sds((8, 128)),
                sds((8, KB)), last,
            ),
            out_specs=(*[vmem()] * 4, smem(), *[vmem()] * 3),
            scratch_shapes=[
                pltpu.VMEM((HALF + 1, KB, 128), BF16), pltpu.VMEM((128, QR), BF16),
                pltpu.VMEM((1, QR), F32), pltpu.VMEM((1, QR), F32),
                *[pltpu.VMEM((KB, TQ), F32)] * 4, pltpu.VMEM((256, QR), BF16),
            ],
            name=name,
        )

    mn, dn, *parts_near, sums, vn, ml = stats(stats_near_kernel, sds((8, QR)), "statsnear")(
        *msgs, qaug, ct, rowmeta, st
    )
    mf, df, *parts_far, _, vf, send = stats(stats_far_kernel, sds((NKEYS, 2, QR)), "statsfar")(
        *onward, qaug, ct, rowmeta, ml, sums
    )
    recv = lax.all_to_all(send, KEYS, 0, 0, tiled=True)
    h, dd, gs = call(
        student_kernel,
        out_shape=(
            sds((STATE, STATE)), sds((8, QR)),
            sds((HALF, STATE, 2 * STATE)),
        ),
        scratch_shapes=[pltpu.VMEM((256, QR), BF16)],
        name="student",
    )(parts_near[1], parts_far[1], vn, vf, qaug, kd, own, st, rowmeta, ct, bt)
    scal, aug, g, eo = call(
        scale_kernel,
        out_shape=(
            sds((NKEYS, 8, 128)), sds((16, QR), BF16), sds((STATE, STATE)),
            sds((16, TQ)),
        ),
        name="scale",
    )(recv, st, dd, rowmeta, ct, mn, mf, dn, df, gs, h)
    scal = lax.all_to_all(scal, KEYS, 0, 0, tiled=True)

    def shared(parts, v):
        kaug, bts, nb = parts
        return nb, kaug, bts, h, v, qaug, aug, ct, rowmeta, eo

    scratch = [
        pltpu.VMEM((256, QR), BF16), pltpu.VMEM((HALF + 1, STATE, KB), F32),
        *[pltpu.VMEM((KB, TQ), F32)] * 2, *[pltpu.VMEM((KB, TQ), BF16)] * 4,
    ]
    o, gb = call(
        own_kernel,
        out_shape=(sds((STATE, QR)), sds((STATE, KB))),
        scratch_shapes=[pltpu.VMEM((256, QR), BF16)],
        name="own",
    )(qaug, aug, kd, bt, own, ct, rowmeta)
    block = sds((2 * STATE + 8, KB))
    *far, o = call(
        far_kernel,
        in_specs=[smem(), *[vmem()] * 11],
        out_shape=(block, block, sds((STATE, QR))),
        scratch_shapes=scratch,
        name="far",
    )(*shared(parts_far, vf), scal, o)
    far = [lax.ppermute(g, ROWS, [(b, a) for a, b in ONWARD]) for g in far]
    *near, gc = call(
        near_kernel,
        in_specs=[smem(), *[vmem()] * 12],
        out_shape=(block, block, sds((NKEYS, STATE, KB))),
        scratch_shapes=[pltpu.VMEM((STATE, QR), F32), *scratch],
        name="near",
    )(*shared(parts_near, vn), scal, o, g)
    gc = lax.all_to_all(gc, KEYS, 0, 0, tiled=True)
    back = [
        lax.ppermute(g + h, BOTH, [(b, a) for a, b in hop])
        for g, h, hop in zip(near, far, HOP_PAIRS)
    ]
    other = functools.reduce(jnp.add, [g[STATE:, :] for g in back])
    other = lax.ppermute(other, KEYS, PAIRS)
    out_c, out_b, out_d = call(
        final_kernel,
        out_shape=(sds((STATE, KB)), sds((STATE, KB)), sds((1, KB))),
        name="final",
    )(*back, other, gb, gc, scal, bt, ct)
    return out_c.T, out_b.T, out_d.reshape(KB)


def solution(mesh):
    return jax.shard_map(
        on_device,
        mesh=mesh,
        in_specs=(
            P(ROWS, None), P(BOTH, None), P(ROWS, None), P(BOTH, None), P(BOTH), P(BOTH),
        ),
        out_specs=(P(BOTH, None), P(BOTH, None), P(BOTH)),
        check_vma=False,
    )
```
